512 devices in a mesh: seq: 128 (over z, x, core), head: 4 (over y).
Axes of the slice: x: 4, y: 4, z: 16, core: 2. Of those that a mesh axis runs over, the one named last changes fastest.
Arguments:
- loader_rows: bfloat16 [65536, 1536], P('seq', 'head'), may hold values from -36 to 36
- plan: int32 [128, 128], replicated, may hold values from 0 to 4, as said below
- lengths: int32 [170], replicated, may hold values from 1 to 1024, 32768 in all
- gain: float32 [1536], replicated, may hold values from 0.1 to 1.9
- wq: bfloat16 [1536, 1536], P(None, 'head'), may hold values from -1.6 to 1.6
- wk: bfloat16 [1536, 1536], P(None, 'head'), may hold values from -1.6 to 1.6
- wv: bfloat16 [1536, 1536], P(None, 'head'), may hold values from -0.15625 to 0.15625
- conv_weight: float32 [31, 1536], P(None, 'head'), may hold values from -1 to 1
- cotangent: bfloat16 [32768, 1536], P('seq', 'head'), may hold values from -6 to 6
Outputs:
- output: bfloat16 [32768, 1536], P('seq', 'head')
- grad_input: bfloat16 [32768, 1536], P('seq', 'head')
The draws below stay inside these ranges and needn't reach their ends.
Inputs may be any that keep to these rules, and one draw needn't show every extreme that they name: plan[s, d] rows go from loader shard s to frame shard d, taken from the start of block (s, d); every row and every column of the plan sums to 256 and holds the same counts as every other row and column, in another order; some entries equal 4. `lengths`: the utterances cover the 32768 frames in order; the longest has exactly 1024 frames.
All inputs are finite; a program needn't handle non-finite values.
Results may differ from the reference program's by a relative error of at most 0.024.
The reference program's roundings to bfloat16 on the way count: a program that leaves them out, or rounds other values in their place, can miss the bound.
Values may be sent and summed in bfloat16 or wider, within the bound.
A program may use at most 64 MiB of HBM per device.

```python
import math
import jax
import jax.numpy as jnp
import numpy as np
from jax import lax

D = 1536
HEADS = 24
HEAD_DIM = 64
KS = 31
HALF_K = 15
WIN = 256
FRAMES = 256
MOST = 1024
CAP = 4
TOTAL = 32768
UTTS = 170
N_SEQ = 128


def draw_loader_rows(key, part):
    row_count = N_SEQ * N_SEQ * CAP
    base_key = jax.random.fold_in(key, 11)
    row_key = jax.random.fold_in(key, 12)
    column_key = jax.random.fold_in(key, 13)
    entries = jnp.clip(jax.random.normal(base_key, (row_count, D), jnp.float32), -4.0, 4.0)
    row_scale = jnp.exp(jax.random.uniform(row_key, (row_count, 1), jnp.float32, math.log(0.3), math.log(3.0)))
    column_scale = jnp.exp(jax.random.uniform(column_key, (1, D), jnp.float32, math.log(0.3), math.log(3.0)))
    return (entries * row_scale * column_scale).astype(jnp.bfloat16)


def draw_plan(key, part):
    half_count = N_SEQ // 2
    low_counts = jax.random.randint(jax.random.fold_in(key, 21), (half_count,), 0, CAP + 1)
    low_counts = low_counts.at[0].set(CAP)
    pattern = jnp.concatenate([low_counts, CAP - low_counts])
    pattern = pattern[jax.random.permutation(jax.random.fold_in(key, 22), N_SEQ)]
    dest_order = jax.random.permutation(jax.random.fold_in(key, 23), N_SEQ)
    source_order = jax.random.permutation(jax.random.fold_in(key, 24), N_SEQ)
    offset = (dest_order[None, :] - source_order[:, None]) % N_SEQ
    return pattern[offset].astype(jnp.int32)


def projection_base(key, salt):
    return jnp.clip(jax.random.normal(jax.random.fold_in(key, salt), (D, D), jnp.float32), -4.0, 4.0) * D ** (-0.5)


def draw_wq(key, part):
    matrix = projection_base(key, 41)
    return matrix.astype(jnp.bfloat16)


def draw_wk(key, part):
    matrix = projection_base(key, 42)
    return matrix.astype(jnp.bfloat16)


def levels(key, dims, split, low, top_value):
    def one(position, parts):
        draws = jax.random.uniform(jax.random.fold_in(jax.random.fold_in(key, 6), position), (parts,), jnp.float32, low / len(split), top_value / len(split))
        return jnp.repeat(jnp.exp(draws), dims[position] // parts).reshape((-1,) + (1,) * (len(dims) - position - 1))

    loudness = one(*split[0])
    for cut in split[1:]:
        loudness = loudness * one(*cut)
    return loudness


def split_up(count, total, limit, lean):
    weights = [(1 << 20) // math.isqrt(grade ** lean) + 1 for grade in range(2, count + 1)]
    spare, holding = total - limit - (count - 1), [1] * (count - 1)
    while spare > 0:
        free = [i for i in range(count - 1) if holding[i] < limit]
        whole, budget = sum([weights[i] for i in free]), spare
        for i in free:
            addition = min(limit - holding[i], max(1, budget * weights[i] // whole), spare)
            holding[i] = holding[i] + addition
            spare = spare - addition
    return np.array([limit] + holding)


def uneven(own_key, count, total, limit, slope):
    if count == 2:
        one = jax.random.randint(own_key, (), max(1, total - limit), min(limit, total - 1) + 1)
        return jnp.stack([one, total - one])
    tallies = jnp.asarray(split_up(count, total, limit, slope), jnp.int32)
    pairs = (count - 1) // 2
    donor, taker = tallies[1:1 + 2 * pairs:2], tallies[2:2 + 2 * pairs:2]
    room = jnp.minimum(donor - 1, limit - taker)
    moved = jax.random.randint(jax.random.fold_in(own_key, 1), (pairs,), 0, 1 << 20) % (room + 1)
    tallies = tallies.at[1:1 + 2 * pairs:2].set(donor - moved).at[2:2 + 2 * pairs:2].set(taker + moved)
    return tallies[jax.random.permutation(jax.random.fold_in(own_key, 2), count)]


def normal_values(stream_key, shape, deviation, most, split=(), kind=jnp.bfloat16):
    level = levels(stream_key, shape, split, -0.22, 0.18) if split else 1.0
    values = jax.random.normal(stream_key, shape, jnp.float32) * deviation * level
    return jnp.minimum(jnp.maximum(values, -most), most).astype(kind)


def setup_inputs(seed: int = 0) -> dict:
    streams_of = jax.random.split(jax.random.key(seed), 10)
    return {
        "loader_rows": draw_loader_rows(jax.random.fold_in(streams_of[9], 71), 0),
        "plan": draw_plan(jax.random.fold_in(streams_of[9], 71), 0),
        "lengths": uneven(streams_of[2], UTTS, TOTAL, MOST, 2).astype(jnp.int32),
        "gain": jnp.clip(1.0 + 0.18 * jax.random.normal(streams_of[3], (D,), jnp.float32), 0.1, 1.9),
        "wq": draw_wq(jax.random.fold_in(streams_of[9], 71), 0),
        "wk": draw_wk(jax.random.fold_in(streams_of[9], 71), 0),
        "wv": normal_values(streams_of[6], (D, D), D ** -0.5, 0.15625, ((1, 4),)),
        "conv_weight": normal_values(streams_of[7], (KS, D), KS ** -0.5, 1.0, ((1, 4),), jnp.float32),
        "cotangent": normal_values(streams_of[8], (TOTAL, D), 1.0, 6.0, ((0, 128), (1, 4))),
    }


EPSILON = 1e-05

def segment_ids(positions, lengths):
    utter_ends = jnp.cumsum(lengths).astype(jnp.int32)
    inside = (positions >= 0) & (positions < TOTAL)
    counted = lax.optimization_barrier(jnp.sum((utter_ends[None, :] <= positions[:, None]).astype(jnp.int32), axis=1))
    return jnp.where(inside, counted, -1).astype(jnp.int32)

def assemble(loader_rows, plan):
    positions = jnp.arange(TOTAL, dtype=jnp.int32)
    owner = positions // FRAMES
    slot_place = positions % FRAMES
    running = jnp.cumsum(plan, axis=0).astype(jnp.int32)
    inclusive = jnp.transpose(running[:, owner])
    exclusive = inclusive - jnp.transpose(plan[:, owner])
    source = lax.optimization_barrier(jnp.sum((inclusive <= slot_place[:, None]).astype(jnp.int32), axis=1))
    already = jnp.take_along_axis(exclusive, source[:, None], axis=1)[:, 0]
    row_index = ((source * N_SEQ + owner) * CAP + slot_place - already).astype(jnp.int32)
    return jnp.take(loader_rows, row_index, axis=0)

def reference(loader_rows, plan, lengths, gain, wq, wk, wv, conv_weight, cotangent):
    score_scale = 1.0 / math.sqrt(HEAD_DIM)
    span = FRAMES + 2 * WIN
    highest = lax.Precision.HIGHEST
    frames = assemble(loader_rows, plan)
    values = frames.astype(jnp.float32)
    row_mean = lax.optimization_barrier(jnp.mean(values, axis=1, keepdims=True))
    centred = values - row_mean
    inverse_std = lax.rsqrt(lax.optimization_barrier(jnp.mean(centred * centred, axis=1, keepdims=True)) + EPSILON)
    unit_rows = centred * inverse_std
    normed = (unit_rows * gain[None, :]).astype(jnp.bfloat16)
    queries = jnp.dot(normed, wq, preferred_element_type=jnp.float32).astype(jnp.bfloat16)
    key_rows = jnp.dot(normed, wk, preferred_element_type=jnp.float32).astype(jnp.bfloat16)
    value_rows = jnp.dot(normed, wv, preferred_element_type=jnp.float32).astype(jnp.bfloat16)
    segments = segment_ids(jnp.arange(-WIN, TOTAL + WIN, dtype=jnp.int32), lengths)
    key_padded = jnp.pad(key_rows, ((WIN, WIN), (0, 0)))
    value_padded = jnp.pad(value_rows, ((WIN, WIN), (0, 0)))
    offset = jnp.arange(span, dtype=jnp.int32)[None, :] - (jnp.arange(FRAMES, dtype=jnp.int32)[:, None] + WIN)
    window_band = (offset >= -WIN) & (offset < WIN)
    starts = jnp.arange(N_SEQ, dtype=jnp.int32) * FRAMES

    def block_weights(block_start):
        query_block = lax.dynamic_slice_in_dim(queries, block_start, FRAMES, 0).reshape(FRAMES, HEADS, HEAD_DIM).astype(jnp.float32)
        key_block = lax.dynamic_slice_in_dim(key_padded, block_start, span, 0).reshape(span, HEADS, HEAD_DIM).astype(jnp.float32)
        value_block = lax.dynamic_slice_in_dim(value_padded, block_start, span, 0).reshape(span, HEADS, HEAD_DIM).astype(jnp.float32)
        seg_block = lax.dynamic_slice_in_dim(segments, block_start, span, 0)
        allowed = window_band & (seg_block[None, :] == seg_block[WIN:WIN + FRAMES][:, None])
        scores = jnp.einsum('qhe,khe->hqk', query_block, key_block, precision=highest) * score_scale
        masked = jnp.where(allowed[None, :, :], scores, -jnp.inf)
        row_max = lax.optimization_barrier(jnp.max(masked, axis=2, keepdims=True))
        lifted = jnp.exp(masked - row_max)
        weights = lifted / lax.optimization_barrier(jnp.sum(lifted, axis=2, keepdims=True))
        weights_low = lax.optimization_barrier(weights.astype(jnp.bfloat16)).astype(jnp.float32)
        attended_block = jnp.einsum('hqk,khe->qhe', weights_low, value_block, precision=highest)
        return (query_block, key_block, value_block, weights, weights_low, attended_block)

    def forward_block(block_start):
        return block_weights(block_start)[5].reshape(FRAMES, D)
    attended = lax.map(forward_block, starts).reshape(TOTAL, D)
    residual = (values + attended).astype(jnp.bfloat16)
    conv_seg = segments[WIN - HALF_K:WIN + TOTAL + HALF_K]
    frame_seg = segments[WIN:WIN + TOTAL]
    residual_pad = jnp.pad(residual, ((HALF_K, HALF_K), (0, 0)))
    conv_out = jnp.zeros((TOTAL, D), jnp.float32)
    for kernel_tap in range(KS):
        same_seg = (conv_seg[kernel_tap:kernel_tap + TOTAL] == frame_seg)[:, None]
        conv_out = conv_out + jnp.where(same_seg, residual_pad[kernel_tap:kernel_tap + TOTAL].astype(jnp.float32) * conv_weight[kernel_tap][None, :], 0.0)
    sigmoid_gate = jax.nn.sigmoid(conv_out)
    output = (residual.astype(jnp.float32) + conv_out * sigmoid_gate).astype(jnp.bfloat16)
    upstream_all = cotangent.astype(jnp.float32)
    grad_conv = (upstream_all * sigmoid_gate * (1.0 + conv_out * (1.0 - sigmoid_gate))).astype(jnp.bfloat16)
    grad_pad = jnp.pad(grad_conv, ((HALF_K, HALF_K), (0, 0)))
    transposed = jnp.zeros((TOTAL, D), jnp.float32)
    for kernel_tap in range(KS):
        mirror = KS - 1 - kernel_tap
        same_seg = (conv_seg[mirror:mirror + TOTAL] == frame_seg)[:, None]
        transposed = transposed + jnp.where(same_seg, grad_pad[mirror:mirror + TOTAL].astype(jnp.float32) * conv_weight[kernel_tap][None, :], 0.0)
    grad_residual = (upstream_all + transposed).astype(jnp.bfloat16)

    def backward_block(running_grads, block_start):
        query_block, key_block, value_block, weights, weights_low, attended_block = block_weights(block_start)
        upstream = lax.dynamic_slice_in_dim(grad_residual, block_start, FRAMES, 0).reshape(FRAMES, HEADS, HEAD_DIM).astype(jnp.float32)
        row_delta = lax.optimization_barrier(jnp.sum(upstream * attended_block, axis=2))
        grad_weights = jnp.einsum('qhe,khe->hqk', upstream, value_block, precision=highest)
        grad_scores = lax.optimization_barrier((weights * (grad_weights - jnp.transpose(row_delta)[:, :, None]) * score_scale).astype(jnp.bfloat16)).astype(jnp.float32)
        grad_query = jnp.einsum('hqk,khe->qhe', grad_scores, key_block, precision=highest).reshape(FRAMES, D)
        grad_keys = jnp.einsum('hqk,qhe->khe', grad_scores, query_block, precision=highest).reshape(span, D)
        grad_values = jnp.einsum('hqk,qhe->khe', weights_low, upstream, precision=highest).reshape(span, D)
        block_grads = jnp.stack([grad_keys, grad_values], axis=1)
        current = lax.dynamic_slice_in_dim(running_grads, block_start, span, 0)
        running_grads = lax.dynamic_update_slice_in_dim(running_grads, current + block_grads, block_start, 0)
        return (running_grads, grad_query)
    initial = jnp.zeros((TOTAL + 2 * WIN, 2, D), jnp.float32)
    kv_grads, query_grads = lax.scan(backward_block, initial, starts)
    grad_query_low = query_grads.reshape(TOTAL, D).astype(jnp.bfloat16)
    kv_own = kv_grads[WIN:WIN + TOTAL]
    grad_key_low = kv_own[:, 0].astype(jnp.bfloat16)
    grad_value_low = kv_own[:, 1].astype(jnp.bfloat16)
    grad_normed = jnp.dot(grad_query_low, jnp.transpose(wq), preferred_element_type=jnp.float32)
    grad_normed = grad_normed + jnp.dot(grad_key_low, jnp.transpose(wk), preferred_element_type=jnp.float32)
    grad_normed = grad_normed + jnp.dot(grad_value_low, jnp.transpose(wv), preferred_element_type=jnp.float32)
    scaled = grad_normed * gain[None, :]
    mean_term = lax.optimization_barrier(jnp.mean(scaled, axis=1, keepdims=True))
    slope_term = lax.optimization_barrier(jnp.mean(scaled * unit_rows, axis=1, keepdims=True))
    through = inverse_std * (scaled - mean_term - unit_rows * slope_term)
    grad_input = (grad_residual.astype(jnp.float32) + through).astype(jnp.bfloat16)
    return (output, grad_input)
```

```python
import math

import jax
import jax.numpy as jnp
from jax import lax
from jax.sharding import PartitionSpec as P

HEAD_DIM = 64
KS = 31
HALF_K = 15
WIN = 256


EPSILON = 1e-05


def extended_2(shard, sides, width):
    for axis, dim in sides:
        size, length = (lax.axis_size(axis), shard.shape[dim])
        up = [(i, (i + 1) % size) for i in range(size - 1)]
        down = [(j, i) for i, j in up]
        last = lax.slice_in_dim(shard, length - width, length, axis=dim)
        leading = lax.slice_in_dim(shard, 0, width, axis=dim)
        before = lax.ppermute(last, axis, up)
        after = lax.ppermute(leading, axis, down)
        shard = jnp.concatenate([before, shard, after], axis=dim)
    return shard


def from_behind(shard, axis, by):
    size = lax.axis_size(axis)
    pairs = [(i, i + by) for i in range(size) if 0 <= i + by < size]
    return lax.ppermute(shard, axis, pairs)


def segment_ids(positions, lengths, frame_total):
    utter_ends = jnp.cumsum(lengths)
    inside = (positions >= 0) & (positions < frame_total)
    counted = jnp.sum((utter_ends[None, :] <= positions[:, None]).astype(jnp.int32), axis=1)
    return jnp.where(inside, counted, -1)


def back_project(grad_part, weight):
    return lax.dot_general(
        grad_part, weight, (((1,), (1,)), ((), ())), preferred_element_type=jnp.float32
    )


def on_device(loader_rows, plan, lengths, gain, wq, wk, wv, conv_weight, cotangent):
    seq_count = lax.axis_size("seq")
    seq_index = lax.axis_index("seq")
    frames, part_cols = cotangent.shape
    head_count = part_cols // HEAD_DIM
    frame_total = frames * seq_count
    capacity = loader_rows.shape[0] // seq_count
    score_scale = 1.0 / math.sqrt(HEAD_DIM)
    blocks = loader_rows.reshape(seq_count, capacity, part_cols)
    arrived = lax.all_to_all(blocks, "seq", split_axis=0, concat_axis=0, tiled=True)
    counts = lax.dynamic_slice_in_dim(plan, seq_index, 1, 1)[:, 0]
    running = jnp.cumsum(counts)
    slot_index = jnp.arange(frames, dtype=jnp.int32)
    source = jnp.sum((running[None, :] <= slot_index[:, None]).astype(jnp.int32), axis=1)
    earlier = jnp.arange(seq_count, dtype=jnp.int32)[None, :] < source[:, None]
    before = jnp.sum(jnp.where(earlier, counts[None, :], 0), axis=1)
    row_index = source * capacity + slot_index - before
    frame_part = jnp.take(arrived.reshape(seq_count * capacity, part_cols), row_index, axis=0)
    gathered = lax.all_gather(frame_part, "head", axis=1, tiled=True)
    values = gathered.astype(jnp.float32)
    row_mean = jnp.mean(values, axis=1, keepdims=True)
    centred = values - row_mean
    inverse_std = lax.rsqrt(jnp.mean(centred * centred, axis=1, keepdims=True) + EPSILON)
    unit_rows = centred * inverse_std
    normed = (unit_rows * gain[None, :]).astype(jnp.bfloat16)
    queries = jnp.dot(normed, wq, preferred_element_type=jnp.float32).astype(jnp.bfloat16)
    key_rows = jnp.dot(normed, wk, preferred_element_type=jnp.float32).astype(jnp.bfloat16)
    value_rows = jnp.dot(normed, wv, preferred_element_type=jnp.float32).astype(jnp.bfloat16)
    stacked = jnp.stack([key_rows, value_rows], axis=1)
    extended = extended_2(stacked, (("seq", 0),), WIN)
    span = frames + 2 * WIN
    key_heads = extended[:, 0].reshape(span, head_count, HEAD_DIM)
    value_heads = extended[:, 1].reshape(span, head_count, HEAD_DIM)
    query_heads = queries.reshape(frames, head_count, HEAD_DIM)
    positions = seq_index * frames + jnp.arange(-WIN, frames + WIN, dtype=jnp.int32)
    segments = segment_ids(positions, lengths, frame_total)
    query_seg = segments[WIN : WIN + frames]
    offset = jnp.arange(span, dtype=jnp.int32)[None, :] - (
        jnp.arange(frames, dtype=jnp.int32)[:, None] + WIN
    )
    allowed = (offset >= -WIN) & (offset < WIN) & (segments[None, :] == query_seg[:, None])
    scores = (
        jnp.einsum("qhe,khe->hqk", query_heads, key_heads, preferred_element_type=jnp.float32)
        * score_scale
    )
    masked = jnp.where(allowed[None, :, :], scores, -jnp.inf)
    row_max = jnp.max(masked, axis=2, keepdims=True)
    lifted = jnp.exp(masked - row_max)
    row_total = jnp.sum(lifted, axis=2, keepdims=True)
    weights = lifted / row_total
    weights_low = weights.astype(jnp.bfloat16)
    attended = jnp.einsum(
        "hqk,khe->qhe", weights_low, value_heads, preferred_element_type=jnp.float32
    )
    residual = (frame_part.astype(jnp.float32) + attended.reshape(frames, part_cols)).astype(
        jnp.bfloat16
    )
    conv_seg = segments[WIN - HALF_K : WIN + frames + HALF_K]
    residual_pad = extended_2(residual, (("seq", 0),), HALF_K)
    conv_out = jnp.zeros((frames, part_cols), jnp.float32)
    for kernel_tap in range(KS):
        same_seg = (conv_seg[kernel_tap : kernel_tap + frames] == query_seg)[:, None]
        conv_out = conv_out + jnp.where(
            same_seg,
            residual_pad[kernel_tap : kernel_tap + frames].astype(jnp.float32)
            * conv_weight[kernel_tap][None, :],
            0.0,
        )
    sigmoid_gate = jax.nn.sigmoid(conv_out)
    output = (residual.astype(jnp.float32) + conv_out * sigmoid_gate).astype(jnp.bfloat16)
    upstream_all = cotangent.astype(jnp.float32)
    grad_conv = (upstream_all * sigmoid_gate * (1.0 + conv_out * (1.0 - sigmoid_gate))).astype(
        jnp.bfloat16
    )
    grad_pad = extended_2(grad_conv, (("seq", 0),), HALF_K)
    transposed = jnp.zeros((frames, part_cols), jnp.float32)
    for kernel_tap in range(KS):
        mirror = KS - 1 - kernel_tap
        same_seg = (conv_seg[mirror : mirror + frames] == query_seg)[:, None]
        transposed = transposed + jnp.where(
            same_seg,
            grad_pad[mirror : mirror + frames].astype(jnp.float32)
            * conv_weight[kernel_tap][None, :],
            0.0,
        )
    grad_residual = (upstream_all + transposed).astype(jnp.bfloat16)
    upstream = grad_residual.reshape(frames, head_count, HEAD_DIM)
    row_delta = jnp.sum(upstream.astype(jnp.float32) * attended, axis=2)
    grad_weights = jnp.einsum(
        "qhe,khe->hqk", upstream, value_heads, preferred_element_type=jnp.float32
    )
    grad_scores = (
        weights * (grad_weights - jnp.transpose(row_delta)[:, :, None]) * score_scale
    ).astype(jnp.bfloat16)
    grad_query = (
        jnp.einsum("hqk,khe->qhe", grad_scores, key_heads, preferred_element_type=jnp.float32)
        .reshape(frames, part_cols)
        .astype(jnp.bfloat16)
    )
    grad_keys = jnp.einsum(
        "hqk,qhe->khe", grad_scores, query_heads, preferred_element_type=jnp.float32
    ).reshape(span, part_cols)
    grad_values = jnp.einsum(
        "hqk,qhe->khe", weights_low, upstream, preferred_element_type=jnp.float32
    ).reshape(span, part_cols)
    kv_grads = jnp.stack([grad_keys, grad_values], axis=1)
    kv_sent = kv_grads.astype(jnp.bfloat16)
    from_right = from_behind(kv_sent[:WIN], "seq", -1)
    from_left = from_behind(kv_sent[frames + WIN :], "seq", 1)
    own_grads = kv_grads[WIN : WIN + frames]
    own_grads = own_grads + from_left.astype(jnp.float32)
    own_grads = own_grads + from_right.astype(jnp.float32)
    grad_key_low = own_grads[:, 0].astype(jnp.bfloat16)
    grad_value_low = own_grads[:, 1].astype(jnp.bfloat16)
    grad_normed = (
        back_project(grad_query, wq)
        + back_project(grad_key_low, wk)
        + back_project(grad_value_low, wv)
    )
    parts = lax.axis_size("head")
    scaled_part = grad_normed * gain[None, :]
    sums = jnp.stack([jnp.sum(scaled_part, axis=1), jnp.sum(scaled_part * unit_rows, axis=1)])
    sums_all = lax.all_to_all(
        jnp.broadcast_to(sums[None], (parts,) + sums.shape), "head", split_axis=0, concat_axis=0, tiled=True
    )
    means = jnp.sum(sums_all, axis=0) / scaled_part.shape[1]
    chunks = jnp.transpose(
        scaled_part.astype(jnp.bfloat16).reshape(frames, parts, part_cols), (1, 0, 2)
    )
    arrived_parts = lax.all_to_all(chunks, "head", split_axis=0, concat_axis=0, tiled=True)
    scaled = jnp.sum(arrived_parts.astype(jnp.float32), axis=0)
    unit_part = (frame_part.astype(jnp.float32) - row_mean) * inverse_std
    through = inverse_std * (scaled - means[0][:, None] - unit_part * means[1][:, None])
    grad_input = (grad_residual.astype(jnp.float32) + through).astype(jnp.bfloat16)
    return (output, grad_input)


def solution(mesh):
    placed = (
        P("seq", "head"),
        P(),
        P(),
        P(),
        P(None, "head"),
        P(None, "head"),
        P(None, "head"),
        P(None, "head"),
        P("seq", "head"),
    )
    return jax.shard_map(
        on_device,
        mesh=mesh,
        in_specs=placed,
        out_specs=(P("seq", "head"), P("seq", "head")),
        check_vma=False,
    )
```

```python
import math

import jax
import jax.numpy as jnp
from jax import lax
from jax.experimental import pallas as pl
from jax.experimental.pallas import tpu as pltpu
from jax.sharding import PartitionSpec as P

HEAD_DIM = 64
KS = 31
HALF_K = 15
WIN = 256
F = 256
PART = 384
GROUPS = 3
LANES = 128
HEADS_ALL = 4
CHUNK = 64
PAD = 16


EPSILON = 1e-05
MESH = pl.DeviceIdType.MESH


def segment_ids(positions, lengths, frame_total):
    utter_ends = jnp.cumsum(lengths)
    inside = (positions >= 0) & (positions < frame_total)
    counted = jnp.sum((utter_ends[None, :] <= positions[:, None]).astype(jnp.int32), axis=1)
    return jnp.where(inside, counted, -1)


def mm(a, b):
    return jnp.dot(a, b, preferred_element_type=jnp.float32)


def mm_nt(a, b):
    return lax.dot_general(a, b, (((1,), (1,)), ((), ())), preferred_element_type=jnp.float32)


def mm_tn(a, b):
    return lax.dot_general(a, b, (((0,), (0,)), ((), ())), preferred_element_type=jnp.float32)


def block_kernel(
    frame_ref, seg_row, seg_col, gain_ref, cw_ref, cot_ref, wq_hbm, wk_hbm, wv_hbm,
    out_ref, grad_ref,
    gath, unit, normed, inv_ref, wq, wk, wv, kv, qs, bias, wts, wlow, att,
    res_low, res_ext, res_halo, gc_low, gc_ext, gc_halo, gres,
    dq_ref, dsend, drecv, down, dkb, dvb, pacc, psend, precv, ssend, srecv,
    w_sem, ag_send, ag_recv, kv_send, kv_recv, rh_send, rh_recv, gh_send, gh_recv,
    d_send, d_recv, p_send, p_recv, s_send, s_recv,
):
    seq_count = lax.axis_size("seq")
    me = lax.axis_index("head")
    seq = lax.axis_index("seq")
    right = lax.rem(seq + 1, seq_count)
    left = lax.rem(seq + seq_count - 1, seq_count)
    scale = 1.0 / math.sqrt(HEAD_DIM)
    f32, bf16 = jnp.float32, jnp.bfloat16

    def peer(off):
        return lax.rem(me + off, HEADS_ALL)

    def remote(src, dst, send, recv, where):
        return pltpu.make_async_remote_copy(
            src_ref=src, dst_ref=dst, send_sem=send, recv_sem=recv, device_id=where, device_id_type=MESH
        )

    loads = [
        pltpu.make_async_copy(src, dst, w_sem.at[i])
        for i, (src, dst) in enumerate(((wk_hbm, wk), (wv_hbm, wv), (wq_hbm, wq)))
    ]
    for copy in loads:
        copy.start()

    barrier = pltpu.get_barrier_semaphore()
    for off in (1, 2, 3):
        pl.semaphore_signal(barrier, inc=1, device_id={"head": peer(off)}, device_id_type=MESH)
    for side in (left, right):
        pl.semaphore_signal(barrier, inc=1, device_id={"seq": side}, device_id_type=MESH)
    pl.semaphore_wait(barrier, 5)

    gathers = [
        remote(frame_ref, gath.at[me], ag_send.at[off - 1], ag_recv.at[off - 1], {"head": peer(off)})
        for off in (2, 1, 3)
    ]
    for copy in gathers:
        copy.start()
    gath[me] = frame_ref[...]

    rows_i = lax.broadcasted_iota(jnp.int32, (F, F), 0)
    cols_i = lax.broadcasted_iota(jnp.int32, (F, F), 1)
    own_seg = seg_col[WIN : WIN + F, 0:1]
    for b in range(3):
        ok = seg_row[:, b * F : (b + 1) * F] == own_seg
        if b == 0:
            ok = ok & (cols_i >= rows_i)
        if b == 2:
            ok = ok & (cols_i < rows_i)
        bias[b] = jnp.where(ok, 0.0, -jnp.inf)

    lane = lax.broadcasted_iota(jnp.int32, (1, LANES), 1)
    mf = [(lane < HEAD_DIM).astype(f32), (lane >= HEAD_DIM).astype(f32)]
    mb = [m.astype(bf16) for m in mf]

    for copy in gathers:
        copy.wait_recv()

    def norm_rows(r, carry):
        rows = pl.ds(pl.multiple_of(r * 32, 32), 32)
        xs = [gath[h, rows, :].astype(f32) for h in range(HEADS_ALL)]
        total = sum(jnp.sum(x, axis=1, keepdims=True) for x in xs)
        mean = total * (1.0 / (HEADS_ALL * PART))
        xs = [x - mean for x in xs]
        square = sum(jnp.sum(x * x, axis=1, keepdims=True) for x in xs)
        inv = lax.rsqrt(square * (1.0 / (HEADS_ALL * PART)) + EPSILON)
        inv_ref[rows, :] = jnp.broadcast_to(inv, (32, LANES))
        for h in range(HEADS_ALL):
            u = xs[h] * inv
            unit[h, rows, :] = u
            normed[rows, h * PART : (h + 1) * PART] = (u * gain_ref[h]).astype(bf16)
        return carry

    lax.fori_loop(0, F // 32, norm_rows, 0)

    halos = []
    for which, weight in ((0, wk), (1, wv)):
        loads[which].wait()
        rows = mm(normed[...], weight[...]).astype(bf16)
        for g in range(GROUPS):
            kv[1, which, g] = rows[:, g * LANES : (g + 1) * LANES]
        halos.append(
            remote(kv.at[1, which], kv.at[2, which], kv_send.at[which, 0], kv_recv.at[which, 0], {"seq": left})
        )
        halos.append(
            remote(kv.at[1, which], kv.at[0, which], kv_send.at[which, 1], kv_recv.at[which, 1], {"seq": right})
        )
        halos[-2].start()
        halos[-1].start()
    loads[2].wait()
    rows = mm(normed[...], wq[...]).astype(bf16)
    for g in range(GROUPS):
        qs[g] = rows[:, g * LANES : (g + 1) * LANES]

    def own_scores(g, carry):
        for sub in range(2):
            wts[2 * g + sub, 1] = mm_nt(qs[g] * mb[sub], kv[1, 0, g]) * scale + bias[1]
        return carry

    lax.fori_loop(0, GROUPS, own_scores, 0)
    for copy in halos:
        copy.wait_recv()

    def attend(g, carry):
        parts = []
        for sub in range(2):
            qm = qs[g] * mb[sub]
            score = [
                mm_nt(qm, kv[0, 0, g]) * scale + bias[0],
                wts[2 * g + sub, 1],
                mm_nt(qm, kv[2, 0, g]) * scale + bias[2],
            ]
            top = jnp.maximum(jnp.maximum(score[0], score[1]), score[2])
            top = jnp.max(top, axis=1, keepdims=True)
            lifted = [jnp.exp(x - top) for x in score]
            total = jnp.sum(lifted[0] + lifted[1] + lifted[2], axis=1, keepdims=True)
            inv = 1.0 / total
            acc = None
            for b in range(3):
                w = lifted[b] * inv
                wts[2 * g + sub, b] = w
                low = w.astype(bf16)
                wlow[2 * g + sub, b] = low
                term = mm(low, kv[b, 1, g])
                acc = term if acc is None else acc + term
            parts.append(acc * mf[sub])
        both = parts[0] + parts[1]
        att[g] = both
        columns = pl.ds(pl.multiple_of(g * LANES, LANES), LANES)
        res = (frame_ref[:, columns].astype(f32) + both).astype(bf16)
        res_low[g] = res
        res_ext[g, PAD : PAD + F, :] = res.astype(f32)
        return carry

    lax.fori_loop(0, GROUPS, attend, 0)

    def edges(low, halo, send, recv):
        return [
            remote(low.at[:, 0:PAD, :], halo.at[1], send.at[0], recv.at[0], {"seq": left}),
            remote(low.at[:, F - PAD : F, :], halo.at[0], send.at[1], recv.at[1], {"seq": right}),
        ]

    def place(halo, ext):
        for g in range(GROUPS):
            ext[g, 0:PAD, :] = halo[0, g].astype(f32)
            ext[g, PAD + F : 2 * PAD + F, :] = halo[1, g].astype(f32)

    res_edges = edges(res_low, res_halo, rh_send, rh_recv)
    for copy in res_edges:
        copy.start()

    def taps(ext, g, r, mirrored):
        base = seg_col[WIN + r : WIN + r + CHUNK, :]
        acc = jnp.zeros((CHUNK, LANES), f32)
        for t in range(KS):
            shift = (HALF_K - t) if mirrored else (t - HALF_K)
            same = seg_col[WIN + r + shift : WIN + r + shift + CHUNK, :] == base
            term = ext[g, PAD + r + shift : PAD + r + shift + CHUNK, :] * cw_ref[g, t : t + 1, :]
            acc = acc + jnp.where(same, term, 0.0)
        return acc

    def forward_conv(starts):
        def body(g, carry):
            columns = pl.ds(pl.multiple_of(g * LANES, LANES), LANES)
            for r in starts:
                conv = taps(res_ext, g, r, False)
                gate = lax.logistic(conv)
                out_ref[r : r + CHUNK, columns] = (
                    res_ext[g, PAD + r : PAD + r + CHUNK, :] + conv * gate
                ).astype(bf16)
                up = cot_ref[r : r + CHUNK, columns].astype(f32)
                gc = (up * gate * (1.0 + conv * (1.0 - gate))).astype(bf16)
                gc_low[g, r : r + CHUNK, :] = gc
                gc_ext[g, PAD + r : PAD + r + CHUNK, :] = gc.astype(f32)
            return carry

        lax.fori_loop(0, GROUPS, body, 0)

    def backward_conv(starts):
        def body(g, carry):
            columns = pl.ds(pl.multiple_of(g * LANES, LANES), LANES)
            for r in starts:
                moved = taps(gc_ext, g, r, True)
                up = cot_ref[r : r + CHUNK, columns].astype(f32)
                gres[g, r : r + CHUNK, :] = (up + moved).astype(bf16)
            return carry

        lax.fori_loop(0, GROUPS, body, 0)

    inner = (CHUNK, 2 * CHUNK)
    outer = (0, 3 * CHUNK)
    forward_conv(inner)
    for copy in res_edges:
        copy.wait_recv()
    place(res_halo, res_ext)
    forward_conv(outer)
    gc_edges = edges(gc_low, gc_halo, gh_send, gh_recv)
    for copy in gc_edges:
        copy.start()
    backward_conv(inner)
    for copy in gc_edges:
        copy.wait_recv()
    place(gc_halo, gc_ext)
    backward_conv(outer)

    def kv_grad_copies(g):
        return [
            remote(dsend.at[0, g], drecv.at[1, g], d_send.at[0, g], d_recv.at[1, g], {"seq": left}),
            remote(dsend.at[1, g], drecv.at[0, g], d_send.at[1, g], d_recv.at[0, g], {"seq": right}),
        ]

    def attend_back(g, carry):
        gq = []
        dk = [None, None, None]
        dv = [None, None, None]
        for sub in range(2):
            gm = gres[g] * mb[sub]
            qm = qs[g] * mb[sub]
            delta = jnp.sum(gm.astype(f32) * att[g], axis=1, keepdims=True)
            acc = None
            for b in range(3):
                gw = mm_nt(gm, kv[b, 1, g])
                ds = (wts[2 * g + sub, b] * (gw - delta) * scale).astype(bf16)
                term = mm(ds, kv[b, 0, g])
                acc = term if acc is None else acc + term
                dkt = mm_tn(ds, qm)
                dvt = mm_tn(wlow[2 * g + sub, b], gm)
                dk[b] = dkt if dk[b] is None else dk[b] + dkt
                dv[b] = dvt if dv[b] is None else dv[b] + dvt
            gq.append(acc * mf[sub])
        columns = pl.ds(pl.multiple_of(g * LANES, LANES), LANES)
        dq_ref[:, columns] = (gq[0] + gq[1]).astype(bf16)
        for slot, b in ((0, 0), (1, 2)):
            dsend[slot, g, 0] = dk[b].astype(bf16)
            dsend[slot, g, 1] = dv[b].astype(bf16)
        down[g, 0] = dk[1]
        down[g, 1] = dv[1]
        for copy in kv_grad_copies(g):
            copy.start()
        return carry

    lax.fori_loop(0, GROUPS, attend_back, 0)

    def weight_rows(ref, off):
        return ref[pl.ds(pl.multiple_of(peer(off) * PART, PART), PART), :]

    for off in (2, 1, 3, 0):
        pacc[off] = mm_nt(dq_ref[...], weight_rows(wq, off))

    for g in range(GROUPS):
        for copy in kv_grad_copies(g):
            copy.wait_recv()
        for which, dst in ((0, dkb), (1, dvb)):
            dst[:, g * LANES : (g + 1) * LANES] = (
                down[g, which] + drecv[0, g, which].astype(f32) + drecv[1, g, which].astype(f32)
            ).astype(bf16)

    row_sum = jnp.zeros((F, 1), f32)
    row_dot = jnp.zeros((F, 1), f32)
    exchanges = []
    for off in (2, 1, 3, 0):
        part = pacc[off] + mm_nt(dkb[...], weight_rows(wk, off)) + mm_nt(dvb[...], weight_rows(wv, off))
        part = part * gain_ref[peer(off)]
        row_sum = row_sum + jnp.sum(part, axis=1, keepdims=True)
        row_dot = row_dot + jnp.sum(part * unit[peer(off)], axis=1, keepdims=True)
        if off:
            psend[off - 1] = part.astype(bf16)
            copy = remote(
                psend.at[off - 1], precv.at[off - 1], p_send.at[off - 1], p_recv.at[off - 1], {"head": peer(off)}
            )
            copy.start()
            exchanges.append(copy)
        else:
            pacc[0] = part

    lanes = lax.broadcasted_iota(jnp.int32, (F, LANES), 1)
    packed = jnp.where(lanes == 0, row_sum, jnp.where(lanes == 1, row_dot, 0.0))
    ssend[...] = jnp.transpose(packed)[0:8, :]
    for off in (2, 1, 3):
        copy = remote(ssend, srecv.at[off - 1], s_send.at[off - 1], s_recv.at[off - 1], {"head": peer(off)})
        copy.start()
        exchanges.append(copy)
    for copy in exchanges:
        copy.wait_recv()
    sums = ssend[...] + srecv[0] + srecv[1] + srecv[2]
    sums = jnp.transpose(jnp.concatenate([sums] * (LANES // 8), axis=0)) * (1.0 / (HEADS_ALL * PART))
    inv_ref[:, 1:2] = sums[:, 0:1]
    inv_ref[:, 2:3] = sums[:, 1:2]

    def finish(r, carry):
        rows = pl.ds(pl.multiple_of(r * 32, 32), 32)
        scaled = pacc[0, rows, :]
        for i in range(3):
            scaled = scaled + precv[i, rows, :].astype(f32)
        through = inv_ref[rows, 0:1] * (
            scaled - inv_ref[rows, 1:2] - unit[me, rows, :] * inv_ref[rows, 2:3]
        )
        for g in range(GROUPS):
            columns = slice(g * LANES, (g + 1) * LANES)
            grad_ref[rows, columns] = (gres[g, rows, :].astype(f32) + through[:, columns]).astype(bf16)
        return carry

    lax.fori_loop(0, F // 32, finish, 0)

    for copy in gathers + halos + res_edges + gc_edges + exchanges:
        copy.wait_send()
    for g in range(GROUPS):
        for copy in kv_grad_copies(g):
            copy.wait_send()


def block_call(frame_part, segments, gain, wq, wk, wv, conv_weight, cotangent):
    f32, bf16 = jnp.float32, jnp.bfloat16
    span = F + 2 * WIN
    seg_row = segments[None, :]
    seg_col = jnp.broadcast_to(segments[:, None], (span, LANES))
    gain_parts = gain.reshape(HEADS_ALL, 1, PART)
    taps = jnp.pad(conv_weight, ((0, 1), (0, 0))).reshape(KS + 1, GROUPS, LANES)
    taps = jnp.transpose(taps, (1, 0, 2))
    vmem = pl.BlockSpec(memory_space=pltpu.VMEM)
    hbm = pl.BlockSpec(memory_space=pl.ANY)
    v = pltpu.VMEM
    dma = pltpu.SemaphoreType.DMA
    shape = jax.ShapeDtypeStruct((F, PART), bf16)
    return pl.pallas_call(
        block_kernel,
        out_shape=(shape, shape),
        in_specs=[vmem] * 6 + [hbm] * 3,
        out_specs=(vmem, vmem),
        scratch_shapes=[
            v((HEADS_ALL, F, PART), bf16),
            v((HEADS_ALL, F, PART), f32),
            v((F, HEADS_ALL * PART), bf16),
            v((F, LANES), f32),
            v((HEADS_ALL * PART, PART), bf16),
            v((HEADS_ALL * PART, PART), bf16),
            v((HEADS_ALL * PART, PART), bf16),
            v((3, 2, GROUPS, F, LANES), bf16),
            v((GROUPS, F, LANES), bf16),
            v((3, F, F), f32),
            v((2 * GROUPS, 3, F, F), f32),
            v((2 * GROUPS, 3, F, F), bf16),
            v((GROUPS, F, LANES), f32),
            v((GROUPS, F, LANES), bf16),
            v((GROUPS, F + 2 * PAD, LANES), f32),
            v((2, GROUPS, PAD, LANES), bf16),
            v((GROUPS, F, LANES), bf16),
            v((GROUPS, F + 2 * PAD, LANES), f32),
            v((2, GROUPS, PAD, LANES), bf16),
            v((GROUPS, F, LANES), bf16),
            v((F, PART), bf16),
            v((2, GROUPS, 2, F, LANES), bf16),
            v((2, GROUPS, 2, F, LANES), bf16),
            v((GROUPS, 2, F, LANES), f32),
            v((F, PART), bf16),
            v((F, PART), bf16),
            v((HEADS_ALL, F, PART), f32),
            v((3, F, PART), bf16),
            v((3, F, PART), bf16),
            v((8, F), f32),
            v((3, 8, F), f32),
            dma((3,)),
            dma((3,)),
            dma((3,)),
            dma((2, 2)),
            dma((2, 2)),
            dma((2,)),
            dma((2,)),
            dma((2,)),
            dma((2,)),
            dma((2, GROUPS)),
            dma((2, GROUPS)),
            dma((3,)),
            dma((3,)),
            dma((3,)),
            dma((3,)),
        ],
        compiler_params=pltpu.CompilerParams(
            collective_id=0, has_side_effects=True, vmem_limit_bytes=56 * 1024 * 1024
        ),
    )(frame_part, seg_row, seg_col, gain_parts, taps, cotangent, wq, wk, wv)


def on_device(loader_rows, plan, lengths, gain, wq, wk, wv, conv_weight, cotangent):
    seq_count = lax.axis_size("seq")
    seq_index = lax.axis_index("seq")
    frames, part_cols = cotangent.shape
    frame_total = frames * seq_count
    capacity = loader_rows.shape[0] // seq_count
    blocks = loader_rows.reshape(seq_count, capacity, part_cols)
    arrived = lax.all_to_all(blocks, "seq", split_axis=0, concat_axis=0, tiled=True)
    counts = lax.dynamic_slice_in_dim(plan, seq_index, 1, 1)[:, 0]
    running = jnp.cumsum(counts)
    slot_index = jnp.arange(frames, dtype=jnp.int32)
    source = jnp.sum((running[None, :] <= slot_index[:, None]).astype(jnp.int32), axis=1)
    earlier = jnp.arange(seq_count, dtype=jnp.int32)[None, :] < source[:, None]
    before = jnp.sum(jnp.where(earlier, counts[None, :], 0), axis=1)
    row_index = source * capacity + slot_index - before
    frame_part = jnp.take(arrived.reshape(seq_count * capacity, part_cols), row_index, axis=0)
    positions = seq_index * frames + jnp.arange(-WIN, frames + WIN, dtype=jnp.int32)
    segments = segment_ids(positions, lengths, frame_total)
    return block_call(frame_part, segments, gain, wq, wk, wv, conv_weight, cotangent)


def solution(mesh):
    placed = (
        P("seq", "head"),
        P(),
        P(),
        P(),
        P(None, "head"),
        P(None, "head"),
        P(None, "head"),
        P(None, "head"),
        P("seq", "head"),
    )
    return jax.shard_map(
        on_device,
        mesh=mesh,
        in_specs=placed,
        out_specs=(P("seq", "head"), P("seq", "head")),
        check_vma=False,
    )
```

```python
import math

import jax
import jax.numpy as jnp
from jax import lax
from jax.experimental import pallas as pl
from jax.experimental.pallas import tpu as pltpu
from jax.sharding import PartitionSpec as P

HEAD_DIM = 64
KS = 31
HALF_K = 15
WIN = 256
F = 256
PART = 384
GROUPS = 3
LANES = 128
HEADS_ALL = 4
CHUNK = 64
PAD = 16


EPSILON = 1e-05
MESH = pl.DeviceIdType.MESH


def mm(a, b):
    return jnp.dot(a, b, preferred_element_type=jnp.float32)


def mm_nt(a, b):
    return lax.dot_general(a, b, (((1,), (1,)), ((), ())), preferred_element_type=jnp.float32)


def mm_tn(a, b):
    return lax.dot_general(a, b, (((0,), (0,)), ((), ())), preferred_element_type=jnp.float32)


def block_kernel(
    plan_ref, len_ref, gain_all, cw_ref, cot_ref, loader, wq_hbm, wk_hbm, wv_hbm,
    out_ref, grad_ref,
    arr, par, hot, len_row, seg_row, seg_col, gain_ref, frame_ref, gath, unit, normed, inv_ref, wq, wk, wv, kv, qs, bias, wts, wlow, att,
    res_low, res_ext, res_halo, gc_low, gc_ext, gc_halo, gres,
    dq_ref, dsend, drecv, down, dkb, dvb, pacc, psend, precv, ssend, srecv,
    a_send, a_recv, f_send, f_recv, own_sem, w_sem, ag_send, ag_recv, kv_send, kv_recv, rh_send, rh_recv, gh_send, gh_recv,
    d_send, d_recv, p_send, p_recv, s_send, s_recv,
):
    seq_count = lax.axis_size("seq")
    me = lax.axis_index("head")
    seq = lax.axis_index("seq")
    right = lax.rem(seq + 1, seq_count)
    left = lax.rem(seq + seq_count - 1, seq_count)
    scale = 1.0 / math.sqrt(HEAD_DIM)
    f32, bf16 = jnp.float32, jnp.bfloat16

    def peer(off):
        return lax.rem(me + off, HEADS_ALL)

    def remote(src, dst, send, recv, where):
        return pltpu.make_async_remote_copy(
            src_ref=src, dst_ref=dst, send_sem=send, recv_sem=recv, device_id=where, device_id_type=MESH
        )

    loads = [
        pltpu.make_async_copy(src, dst, w_sem.at[i])
        for i, (src, dst) in enumerate(((wk_hbm, wk), (wv_hbm, wv), (wq_hbm, wq)))
    ]
    for copy in loads:
        copy.start()

    pairs, tile = loader.shape[0], loader.shape[1]
    slots, capacity = pairs * tile, tile // 2
    half = pairs // 2
    core = lax.rem(seq, 2)
    pair = lax.div(seq, 2)
    partner = seq + 1 - 2 * core
    own_tile = pltpu.make_async_copy(loader.at[pair], arr.at[pair], own_sem.at[0])
    own_tile.start()

    barrier = pltpu.get_barrier_semaphore()

    def greet(j, carry):
        pl.semaphore_signal(
            barrier, inc=1, device_id={"seq": lax.rem(seq + 2 * j, seq_count)}, device_id_type=MESH
        )
        return carry

    lax.fori_loop(1, pairs, greet, 0)
    for off in (1, 2, 3):
        pl.semaphore_signal(barrier, inc=1, device_id={"head": peer(off)}, device_id_type=MESH)
    for side in (left, right, partner):
        pl.semaphore_signal(barrier, inc=1, device_id={"seq": side}, device_id_type=MESH)

    for h in range(HEADS_ALL):
        gain_ref[h] = gain_all[:, h * PART : (h + 1) * PART]
    len_row[...] = jnp.zeros_like(len_row)
    len_row[0:1, 0 : len_ref.shape[1]] = len_ref[...].astype(f32)
    rows_i = lax.broadcasted_iota(jnp.int32, (F, F), 0)
    cols_i = lax.broadcasted_iota(jnp.int32, (F, F), 1)
    pl.semaphore_wait(barrier, pairs + 5)

    def slot_copy(j):
        there = lax.rem(pair + j, pairs)
        return remote(
            loader.at[there], arr.at[pair], a_send.at[j], a_recv.at[j], {"seq": lax.rem(seq + 2 * j, seq_count)}
        )

    def pass_on(j):
        slot = lax.rem(pair + pairs - j, pairs)
        return remote(arr.at[slot], par.at[slot], f_send.at[j], f_recv.at[j], {"seq": partner})

    own_pass = remote(loader.at[pair], par.at[pair], f_send.at[0], f_recv.at[0], {"seq": partner})

    def both_ways(act):
        act(half)

        def body(i, carry):
            act(half - i)
            act(half + i)
            return carry

        lax.fori_loop(1, half, body, 0)

    both_ways(lambda j: slot_copy(j).start())
    own_pass.start()

    lens = len_row[0:1, :]
    ends_col = jnp.sum(jnp.where(cols_i <= rows_i, lens, 0.0), axis=1, keepdims=True)
    lens_col = jnp.transpose(jnp.broadcast_to(lens, (LANES, F)))[:, 0:1]
    ends_row = jnp.sum(jnp.where(rows_i <= cols_i, lens_col, 0.0), axis=0, keepdims=True)
    total = (seq_count * F) * 1.0
    first = (seq * F - WIN).astype(f32)
    for b in range(3):
        place_row = lax.broadcasted_iota(jnp.int32, (1, F), 1).astype(f32) + (first + b * F)
        inside = (place_row >= 0.0) & (place_row < total)
        count = jnp.sum((ends_col <= place_row).astype(f32), axis=0, keepdims=True)
        seg_row[0:1, b * F : (b + 1) * F] = jnp.where(inside, count, -1.0)
        place_col = lax.broadcasted_iota(jnp.int32, (F, 1), 0).astype(f32) + (first + b * F)
        inside = (place_col >= 0.0) & (place_col < total)
        count = jnp.sum((ends_row <= place_col).astype(f32), axis=1, keepdims=True)
        seg_col[b * F : (b + 1) * F, :] = jnp.broadcast_to(jnp.where(inside, count, -1.0), (F, LANES))

    own_seg = seg_col[WIN : WIN + F, 0:1]
    for b in range(3):
        ok = seg_row[0:1, b * F : (b + 1) * F] == own_seg
        if b == 0:
            ok = ok & (cols_i >= rows_i)
        if b == 2:
            ok = ok & (cols_i < rows_i)
        bias[b] = jnp.where(ok, 0.0, -jnp.inf)

    lane = lax.broadcasted_iota(jnp.int32, (1, LANES), 1)
    mf = [(lane < HEAD_DIM).astype(f32), (lane >= HEAD_DIM).astype(f32)]
    mb = [m.astype(bf16) for m in mf]

    chosen = (lax.broadcasted_iota(jnp.int32, (8, seq_count), 1) == seq).astype(f32).astype(bf16)
    counts = mm_nt(chosen, plan_ref[...].astype(f32).astype(bf16)).astype(bf16)
    lower = lax.broadcasted_iota(jnp.int32, (seq_count, seq_count), 0)
    upper = lax.broadcasted_iota(jnp.int32, (seq_count, seq_count), 1)
    starts = mm(counts, (lower < upper).astype(f32).astype(bf16)).astype(bf16)
    loader_row = lax.broadcasted_iota(jnp.int32, (seq_count, slots), 0)
    slot_pair = lax.shift_right_logical(
        lax.broadcasted_iota(jnp.int32, (seq_count, slots), 1), jnp.int32(tile.bit_length() - 1)
    )
    slot_row = lax.broadcasted_iota(jnp.int32, (1, slots), 1)
    slot_core = lax.shift_right_logical(slot_row, jnp.int32(capacity.bit_length() - 1)) & 1
    within = (slot_row & (capacity - 1)).astype(f32)
    frame_rows = lax.broadcasted_iota(jnp.int32, (F, slots), 0).astype(f32)
    for which, parity in ((0, core), (1, 1 - core)):
        spread = (loader_row == 2 * slot_pair + parity).astype(f32).astype(bf16)
        count = mm(counts, spread)[0:1, :]
        start = mm(starts, spread)[0:1, :]
        target = jnp.where((slot_core == core) & (within < count), start + within, -1.0)
        hot[which] = (frame_rows == target).astype(f32).astype(bf16)

    def land(j):
        slot_copy(j).wait_recv()
        pass_on(j).start()

    both_ways(land)
    own_tile.wait()
    own_pass.wait_recv()
    both_ways(lambda j: pass_on(j).wait_recv())
    frame_ref[...] = (
        mm(hot[0], arr[...].reshape(slots, PART)) + mm(hot[1], par[...].reshape(slots, PART))
    ).astype(bf16)

    gathers = [
        remote(frame_ref, gath.at[me], ag_send.at[off - 1], ag_recv.at[off - 1], {"head": peer(off)})
        for off in (2, 1, 3)
    ]
    for copy in gathers:
        copy.start()
    gath[me] = frame_ref[...]

    for copy in gathers:
        copy.wait_recv()

    def norm_rows(r, carry):
        rows = pl.ds(pl.multiple_of(r * 32, 32), 32)
        xs = [gath[h, rows, :].astype(f32) for h in range(HEADS_ALL)]
        total = sum(jnp.sum(x, axis=1, keepdims=True) for x in xs)
        mean = total * (1.0 / (HEADS_ALL * PART))
        xs = [x - mean for x in xs]
        square = sum(jnp.sum(x * x, axis=1, keepdims=True) for x in xs)
        inv = lax.rsqrt(square * (1.0 / (HEADS_ALL * PART)) + EPSILON)
        inv_ref[rows, :] = jnp.broadcast_to(inv, (32, LANES))
        for h in range(HEADS_ALL):
            u = xs[h] * inv
            unit[h, rows, :] = u
            normed[rows, h * PART : (h + 1) * PART] = (u * gain_ref[h]).astype(bf16)
        return carry

    lax.fori_loop(0, F // 32, norm_rows, 0)

    halos = []
    for which, weight in ((0, wk), (1, wv)):
        loads[which].wait()
        rows = mm(normed[...], weight[...]).astype(bf16)
        for g in range(GROUPS):
            kv[1, which, g] = rows[:, g * LANES : (g + 1) * LANES]
        halos.append(
            remote(kv.at[1, which], kv.at[2, which], kv_send.at[which, 0], kv_recv.at[which, 0], {"seq": left})
        )
        halos.append(
            remote(kv.at[1, which], kv.at[0, which], kv_send.at[which, 1], kv_recv.at[which, 1], {"seq": right})
        )
        halos[-2].start()
        halos[-1].start()
    loads[2].wait()
    rows = mm(normed[...], wq[...]).astype(bf16)
    for g in range(GROUPS):
        qs[g] = rows[:, g * LANES : (g + 1) * LANES]

    def own_scores(g, carry):
        for sub in range(2):
            wts[2 * g + sub, 1] = mm_nt(qs[g] * mb[sub], kv[1, 0, g]) * scale + bias[1]
        return carry

    lax.fori_loop(0, GROUPS, own_scores, 0)
    for copy in halos:
        copy.wait_recv()

    def attend(g, carry):
        parts = []
        for sub in range(2):
            qm = qs[g] * mb[sub]
            score = [
                mm_nt(qm, kv[0, 0, g]) * scale + bias[0],
                wts[2 * g + sub, 1],
                mm_nt(qm, kv[2, 0, g]) * scale + bias[2],
            ]
            top = jnp.maximum(jnp.maximum(score[0], score[1]), score[2])
            top = jnp.max(top, axis=1, keepdims=True)
            lifted = [jnp.exp(x - top) for x in score]
            total = jnp.sum(lifted[0] + lifted[1] + lifted[2], axis=1, keepdims=True)
            inv = 1.0 / total
            acc = None
            for b in range(3):
                w = lifted[b] * inv
                wts[2 * g + sub, b] = w
                low = w.astype(bf16)
                wlow[2 * g + sub, b] = low
                term = mm(low, kv[b, 1, g])
                acc = term if acc is None else acc + term
            parts.append(acc * mf[sub])
        both = parts[0] + parts[1]
        att[g] = both
        columns = pl.ds(pl.multiple_of(g * LANES, LANES), LANES)
        res = (frame_ref[:, columns].astype(f32) + both).astype(bf16)
        res_low[g] = res
        res_ext[g, PAD : PAD + F, :] = res.astype(f32)
        return carry

    lax.fori_loop(0, GROUPS, attend, 0)

    def edges(low, halo, send, recv):
        return [
            remote(low.at[:, 0:PAD, :], halo.at[1], send.at[0], recv.at[0], {"seq": left}),
            remote(low.at[:, F - PAD : F, :], halo.at[0], send.at[1], recv.at[1], {"seq": right}),
        ]

    def place(halo, ext):
        for g in range(GROUPS):
            ext[g, 0:PAD, :] = halo[0, g].astype(f32)
            ext[g, PAD + F : 2 * PAD + F, :] = halo[1, g].astype(f32)

    res_edges = edges(res_low, res_halo, rh_send, rh_recv)
    for copy in res_edges:
        copy.start()

    def taps(ext, g, r, mirrored):
        base = seg_col[WIN + r : WIN + r + CHUNK, :]
        acc = jnp.zeros((CHUNK, LANES), f32)
        for t in range(KS):
            shift = (HALF_K - t) if mirrored else (t - HALF_K)
            same = seg_col[WIN + r + shift : WIN + r + shift + CHUNK, :] == base
            term = ext[g, PAD + r + shift : PAD + r + shift + CHUNK, :] * cw_ref[t : t + 1, pl.ds(pl.multiple_of(g * LANES, LANES), LANES)]
            acc = acc + jnp.where(same, term, 0.0)
        return acc

    def forward_conv(starts):
        def body(g, carry):
            columns = pl.ds(pl.multiple_of(g * LANES, LANES), LANES)
            for r in starts:
                conv = taps(res_ext, g, r, False)
                gate = lax.logistic(conv)
                out_ref[r : r + CHUNK, columns] = (
                    res_ext[g, PAD + r : PAD + r + CHUNK, :] + conv * gate
                ).astype(bf16)
                up = cot_ref[r : r + CHUNK, columns].astype(f32)
                gc = (up * gate * (1.0 + conv * (1.0 - gate))).astype(bf16)
                gc_low[g, r : r + CHUNK, :] = gc
                gc_ext[g, PAD + r : PAD + r + CHUNK, :] = gc.astype(f32)
            return carry

        lax.fori_loop(0, GROUPS, body, 0)

    def backward_conv(starts):
        def body(g, carry):
            columns = pl.ds(pl.multiple_of(g * LANES, LANES), LANES)
            for r in starts:
                moved = taps(gc_ext, g, r, True)
                up = cot_ref[r : r + CHUNK, columns].astype(f32)
                gres[g, r : r + CHUNK, :] = (up + moved).astype(bf16)
            return carry

        lax.fori_loop(0, GROUPS, body, 0)

    inner = (CHUNK, 2 * CHUNK)
    outer = (0, 3 * CHUNK)
    forward_conv(inner)
    for copy in res_edges:
        copy.wait_recv()
    place(res_halo, res_ext)
    forward_conv(outer)
    gc_edges = edges(gc_low, gc_halo, gh_send, gh_recv)
    for copy in gc_edges:
        copy.start()
    backward_conv(inner)
    for copy in gc_edges:
        copy.wait_recv()
    place(gc_halo, gc_ext)
    backward_conv(outer)

    def kv_grad_copies(g):
        return [
            remote(dsend.at[0, g], drecv.at[1, g], d_send.at[0, g], d_recv.at[1, g], {"seq": left}),
            remote(dsend.at[1, g], drecv.at[0, g], d_send.at[1, g], d_recv.at[0, g], {"seq": right}),
        ]

    def attend_back(g, carry):
        gq = []
        dk = [None, None, None]
        dv = [None, None, None]
        for sub in range(2):
            gm = gres[g] * mb[sub]
            qm = qs[g] * mb[sub]
            delta = jnp.sum(gm.astype(f32) * att[g], axis=1, keepdims=True)
            acc = None
            for b in range(3):
                gw = mm_nt(gm, kv[b, 1, g])
                ds = (wts[2 * g + sub, b] * (gw - delta) * scale).astype(bf16)
                term = mm(ds, kv[b, 0, g])
                acc = term if acc is None else acc + term
                dkt = mm_tn(ds, qm)
                dvt = mm_tn(wlow[2 * g + sub, b], gm)
                dk[b] = dkt if dk[b] is None else dk[b] + dkt
                dv[b] = dvt if dv[b] is None else dv[b] + dvt
            gq.append(acc * mf[sub])
        columns = pl.ds(pl.multiple_of(g * LANES, LANES), LANES)
        dq_ref[:, columns] = (gq[0] + gq[1]).astype(bf16)
        for slot, b in ((0, 0), (1, 2)):
            dsend[slot, g, 0] = dk[b].astype(bf16)
            dsend[slot, g, 1] = dv[b].astype(bf16)
        down[g, 0] = dk[1]
        down[g, 1] = dv[1]
        for copy in kv_grad_copies(g):
            copy.start()
        return carry

    lax.fori_loop(0, GROUPS, attend_back, 0)

    def weight_rows(ref, off):
        return ref[pl.ds(pl.multiple_of(peer(off) * PART, PART), PART), :]

    for off in (2, 1, 3, 0):
        pacc[off] = mm_nt(dq_ref[...], weight_rows(wq, off))

    for g in range(GROUPS):
        for copy in kv_grad_copies(g):
            copy.wait_recv()
        for which, dst in ((0, dkb), (1, dvb)):
            dst[:, g * LANES : (g + 1) * LANES] = (
                down[g, which] + drecv[0, g, which].astype(f32) + drecv[1, g, which].astype(f32)
            ).astype(bf16)

    row_sum = jnp.zeros((F, 1), f32)
    row_dot = jnp.zeros((F, 1), f32)
    exchanges = []
    for off in (2, 1, 3, 0):
        part = pacc[off] + mm_nt(dkb[...], weight_rows(wk, off)) + mm_nt(dvb[...], weight_rows(wv, off))
        part = part * gain_ref[peer(off)]
        row_sum = row_sum + jnp.sum(part, axis=1, keepdims=True)
        row_dot = row_dot + jnp.sum(part * unit[peer(off)], axis=1, keepdims=True)
        if off:
            psend[off - 1] = part.astype(bf16)
            copy = remote(
                psend.at[off - 1], precv.at[off - 1], p_send.at[off - 1], p_recv.at[off - 1], {"head": peer(off)}
            )
            copy.start()
            exchanges.append(copy)
        else:
            pacc[0] = part

    lanes = lax.broadcasted_iota(jnp.int32, (F, LANES), 1)
    packed = jnp.where(lanes == 0, row_sum, jnp.where(lanes == 1, row_dot, 0.0))
    ssend[...] = jnp.transpose(packed)[0:8, :]
    for off in (2, 1, 3):
        copy = remote(ssend, srecv.at[off - 1], s_send.at[off - 1], s_recv.at[off - 1], {"head": peer(off)})
        copy.start()
        exchanges.append(copy)
    for copy in exchanges:
        copy.wait_recv()
    sums = ssend[...] + srecv[0] + srecv[1] + srecv[2]
    sums = jnp.transpose(jnp.concatenate([sums] * (LANES // 8), axis=0)) * (1.0 / (HEADS_ALL * PART))
    inv_ref[:, 1:2] = sums[:, 0:1]
    inv_ref[:, 2:3] = sums[:, 1:2]

    def finish(r, carry):
        rows = pl.ds(pl.multiple_of(r * 32, 32), 32)
        scaled = pacc[0, rows, :]
        for i in range(3):
            scaled = scaled + precv[i, rows, :].astype(f32)
        through = inv_ref[rows, 0:1] * (
            scaled - inv_ref[rows, 1:2] - unit[me, rows, :] * inv_ref[rows, 2:3]
        )
        for g in range(GROUPS):
            columns = slice(g * LANES, (g + 1) * LANES)
            grad_ref[rows, columns] = (gres[g, rows, :].astype(f32) + through[:, columns]).astype(bf16)
        return carry

    lax.fori_loop(0, F // 32, finish, 0)

    both_ways(lambda j: slot_copy(j).wait_send())
    both_ways(lambda j: pass_on(j).wait_send())
    own_pass.wait_send()
    for copy in gathers + halos + res_edges + gc_edges + exchanges:
        copy.wait_send()
    for g in range(GROUPS):
        for copy in kv_grad_copies(g):
            copy.wait_send()


def block_call(loader_rows, plan, lengths, gain, wq, wk, wv, conv_weight, cotangent):
    f32, bf16 = jnp.float32, jnp.bfloat16
    seq_count = lax.axis_size("seq")
    span = F + 2 * WIN
    pairs = seq_count // 2
    tile = loader_rows.shape[0] // pairs
    slots = pairs * tile
    loader = loader_rows.reshape(pairs, tile, PART)
    vmem = pl.BlockSpec(memory_space=pltpu.VMEM)
    hbm = pl.BlockSpec(memory_space=pl.ANY)
    v = pltpu.VMEM
    dma = pltpu.SemaphoreType.DMA
    shape = jax.ShapeDtypeStruct((F, PART), bf16)
    return pl.pallas_call(
        block_kernel,
        out_shape=(shape, shape),
        in_specs=[vmem] * 5 + [hbm] * 4,
        out_specs=(vmem, vmem),
        scratch_shapes=[
            v((pairs, tile, PART), bf16),
            v((pairs, tile, PART), bf16),
            v((2, F, slots), bf16),
            v((8, F), f32),
            v((8, span), f32),
            v((span, LANES), f32),
            v((HEADS_ALL, 1, PART), f32),
            v((F, PART), bf16),
            v((HEADS_ALL, F, PART), bf16),
            v((HEADS_ALL, F, PART), f32),
            v((F, HEADS_ALL * PART), bf16),
            v((F, LANES), f32),
            v((HEADS_ALL * PART, PART), bf16),
            v((HEADS_ALL * PART, PART), bf16),
            v((HEADS_ALL * PART, PART), bf16),
            v((3, 2, GROUPS, F, LANES), bf16),
            v((GROUPS, F, LANES), bf16),
            v((3, F, F), f32),
            v((2 * GROUPS, 3, F, F), f32),
            v((2 * GROUPS, 3, F, F), bf16),
            v((GROUPS, F, LANES), f32),
            v((GROUPS, F, LANES), bf16),
            v((GROUPS, F + 2 * PAD, LANES), f32),
            v((2, GROUPS, PAD, LANES), bf16),
            v((GROUPS, F, LANES), bf16),
            v((GROUPS, F + 2 * PAD, LANES), f32),
            v((2, GROUPS, PAD, LANES), bf16),
            v((GROUPS, F, LANES), bf16),
            v((F, PART), bf16),
            v((2, GROUPS, 2, F, LANES), bf16),
            v((2, GROUPS, 2, F, LANES), bf16),
            v((GROUPS, 2, F, LANES), f32),
            v((F, PART), bf16),
            v((F, PART), bf16),
            v((HEADS_ALL, F, PART), f32),
            v((3, F, PART), bf16),
            v((3, F, PART), bf16),
            v((8, F), f32),
            v((3, 8, F), f32),
            dma((pairs,)),
            dma((pairs,)),
            dma((pairs,)),
            dma((pairs,)),
            dma((1,)),
            dma((3,)),
            dma((3,)),
            dma((3,)),
            dma((2, 2)),
            dma((2, 2)),
            dma((2,)),
            dma((2,)),
            dma((2,)),
            dma((2,)),
            dma((2, GROUPS)),
            dma((2, GROUPS)),
            dma((3,)),
            dma((3,)),
            dma((3,)),
            dma((3,)),
        ],
        compiler_params=pltpu.CompilerParams(
            collective_id=0, has_side_effects=True, vmem_limit_bytes=56 * 1024 * 1024
        ),
    )(plan, lengths[None, :], gain[None, :], conv_weight, cotangent, loader, wq, wk, wv)


def on_device(loader_rows, plan, lengths, gain, wq, wk, wv, conv_weight, cotangent):
    return block_call(loader_rows, plan, lengths, gain, wq, wk, wv, conv_weight, cotangent)


def solution(mesh):
    placed = (
        P("seq", "head"),
        P(),
        P(),
        P(),
        P(None, "head"),
        P(None, "head"),
        P(None, "head"),
        P(None, "head"),
        P("seq", "head"),
    )
    return jax.shard_map(
        on_device,
        mesh=mesh,
        in_specs=placed,
        out_specs=(P("seq", "head"), P("seq", "head")),
        check_vma=False,
    )
```

```python
import math

import jax
import jax.numpy as jnp
from jax import lax
from jax.experimental import pallas as pl
from jax.experimental.pallas import tpu as pltpu
from jax.sharding import PartitionSpec as P

HEAD_DIM = 64
KS = 31
HALF_K = 15
WIN = 256
F = 256
PART = 384
GROUPS = 3
LANES = 128
HEADS_ALL = 4
CHUNK = 64
PAD = 16


EPSILON = 1e-05
MESH = pl.DeviceIdType.MESH


def mm(a, b):
    return jnp.dot(a, b, preferred_element_type=jnp.float32)


def mm_nt(a, b):
    return lax.dot_general(a, b, (((1,), (1,)), ((), ())), preferred_element_type=jnp.float32)


def mm_tn(a, b):
    return lax.dot_general(a, b, (((0,), (0,)), ((), ())), preferred_element_type=jnp.float32)


def block_kernel(
    plan_ref, len_ref, gain_all, cw_ref, cot_ref, loader, wq_hbm, wk_hbm, wv_hbm,
    out_ref, grad_ref,
    zin, arr, par, hot, len_row, seg_row, seg_col, gain_ref, frame_ref, gath, unit, normed, inv_ref, wq, wk, wv, kv, qs, bias, wts, wlow, att,
    res_low, res_ext, res_halo, gc_low, gc_ext, gc_halo, gres,
    dq_ref, dsend, drecv, down, dkb, dvb, pacc, psend, relay, precv, ssend, srecv,
    z_send, z_recv, x_send, x_recv, l_sem, f_send, f_recv, own_sem, w_sem, ag_send, ag_recv, kv_send, kv_recv, rh_send, rh_recv, gh_send, gh_recv,
    d_send, d_recv, p_send, p_recv, s_send, s_recv,
):
    seq_count = lax.axis_size("seq")
    me = lax.axis_index("head")
    seq = lax.axis_index("seq")
    right = lax.rem(seq + 1, seq_count)
    left = lax.rem(seq + seq_count - 1, seq_count)
    scale = 1.0 / math.sqrt(HEAD_DIM)
    f32, bf16 = jnp.float32, jnp.bfloat16

    def peer(off):
        return lax.rem(me + off, HEADS_ALL)

    def remote(src, dst, send, recv, where):
        return pltpu.make_async_remote_copy(
            src_ref=src, dst_ref=dst, send_sem=send, recv_sem=recv, device_id=where, device_id_type=MESH
        )

    loads = [
        pltpu.make_async_copy(src, dst, w_sem.at[i])
        for i, (src, dst) in enumerate(((wk_hbm, wk), (wv_hbm, wv), (wq_hbm, wq)))
    ]
    for copy in loads:
        copy.start()

    deep, wide, tile = loader.shape[0], loader.shape[1], loader.shape[2]
    slots, capacity = deep * wide * tile, tile // 2
    core = lax.rem(seq, 2)
    pair = lax.div(seq, 2)
    z, x = lax.div(pair, wide), lax.rem(pair, wide)
    partner = seq + 1 - 2 * core
    own_tile = pltpu.make_async_copy(loader.at[z], zin.at[z], own_sem.at[0])
    own_tile.start()
    order = sorted(range(1, deep), key=lambda j: -min(j, deep - j))

    def at_z(j):
        return (lax.rem(z + j, deep) * wide + x) * 2 + core

    def at_x(k):
        return (z * wide + lax.rem(x + k, wide)) * 2 + core

    barrier = pltpu.get_barrier_semaphore()
    for j in order:
        pl.semaphore_signal(barrier, inc=1, device_id={"seq": at_z(j)}, device_id_type=MESH)
    for k in range(1, wide):
        pl.semaphore_signal(barrier, inc=1, device_id={"seq": at_x(k)}, device_id_type=MESH)
    for off in (1, 2, 3):
        pl.semaphore_signal(barrier, inc=1, device_id={"head": peer(off)}, device_id_type=MESH)
    for side in (left, right, partner):
        pl.semaphore_signal(barrier, inc=1, device_id={"seq": side}, device_id_type=MESH)

    for h in range(HEADS_ALL):
        gain_ref[h] = gain_all[:, h * PART : (h + 1) * PART]
    len_row[...] = jnp.zeros_like(len_row)
    len_row[0:1, 0 : len_ref.shape[1]] = len_ref[...].astype(f32)
    rows_i = lax.broadcasted_iota(jnp.int32, (F, F), 0)
    cols_i = lax.broadcasted_iota(jnp.int32, (F, F), 1)
    pl.semaphore_wait(barrier, deep + wide + 4)

    def far(j):
        return remote(
            loader.at[lax.rem(z + j, deep)], zin.at[z], z_send.at[j], z_recv.at[j], {"seq": at_z(j)}
        )

    def spread_out(j):
        layer = lax.rem(z + deep - j, deep)
        return [
            remote(
                zin.at[layer, lax.rem(x + k, wide)], arr.at[layer, x],
                x_send.at[j, k], x_recv.at[j, k], {"seq": at_x(k)},
            )
            for k in range(1, wide)
        ]

    def keep(j):
        layer = lax.rem(z + deep - j, deep)
        return pltpu.make_async_copy(zin.at[layer, x], arr.at[layer, x], l_sem.at[j])

    def pass_on(j):
        layer = lax.rem(z + deep - j, deep)
        return remote(arr.at[layer], par.at[layer], f_send.at[j], f_recv.at[j], {"seq": partner})

    for j in order:
        far(j).start()
    own_tile.wait()
    keep(0).start()
    for copy in spread_out(0):
        copy.start()

    lens = len_row[0:1, :]
    ends_col = jnp.sum(jnp.where(cols_i <= rows_i, lens, 0.0), axis=1, keepdims=True)
    lens_col = jnp.transpose(jnp.broadcast_to(lens, (LANES, F)))[:, 0:1]
    ends_row = jnp.sum(jnp.where(rows_i <= cols_i, lens_col, 0.0), axis=0, keepdims=True)
    total = (seq_count * F) * 1.0
    first = (seq * F - WIN).astype(f32)
    for b in range(3):
        place_row = lax.broadcasted_iota(jnp.int32, (1, F), 1).astype(f32) + (first + b * F)
        inside = (place_row >= 0.0) & (place_row < total)
        count = jnp.sum((ends_col <= place_row).astype(f32), axis=0, keepdims=True)
        seg_row[0:1, b * F : (b + 1) * F] = jnp.where(inside, count, -1.0)
        place_col = lax.broadcasted_iota(jnp.int32, (F, 1), 0).astype(f32) + (first + b * F)
        inside = (place_col >= 0.0) & (place_col < total)
        count = jnp.sum((ends_row <= place_col).astype(f32), axis=1, keepdims=True)
        seg_col[b * F : (b + 1) * F, :] = jnp.broadcast_to(jnp.where(inside, count, -1.0), (F, LANES))

    own_seg = seg_col[WIN : WIN + F, 0:1]
    for b in range(3):
        ok = seg_row[0:1, b * F : (b + 1) * F] == own_seg
        if b == 0:
            ok = ok & (cols_i >= rows_i)
        if b == 2:
            ok = ok & (cols_i < rows_i)
        bias[b] = jnp.where(ok, 0.0, -jnp.inf)

    lane = lax.broadcasted_iota(jnp.int32, (1, LANES), 1)
    mf = [(lane < HEAD_DIM).astype(f32), (lane >= HEAD_DIM).astype(f32)]
    mb = [m.astype(bf16) for m in mf]

    chosen = (lax.broadcasted_iota(jnp.int32, (8, seq_count), 1) == seq).astype(f32).astype(bf16)
    counts = mm_nt(chosen, plan_ref[...].astype(f32).astype(bf16)).astype(bf16)
    lower = lax.broadcasted_iota(jnp.int32, (seq_count, seq_count), 0)
    upper = lax.broadcasted_iota(jnp.int32, (seq_count, seq_count), 1)
    starts = mm(counts, (lower < upper).astype(f32).astype(bf16)).astype(bf16)
    loader_row = lax.broadcasted_iota(jnp.int32, (seq_count, slots), 0)
    slot_pair = lax.shift_right_logical(
        lax.broadcasted_iota(jnp.int32, (seq_count, slots), 1), jnp.int32(tile.bit_length() - 1)
    )
    slot_row = lax.broadcasted_iota(jnp.int32, (1, slots), 1)
    slot_core = lax.shift_right_logical(slot_row, jnp.int32(capacity.bit_length() - 1)) & 1
    within = (slot_row & (capacity - 1)).astype(f32)
    frame_rows = lax.broadcasted_iota(jnp.int32, (F, slots), 0).astype(f32)
    for which, parity in ((0, core), (1, 1 - core)):
        spread = (loader_row == 2 * slot_pair + parity).astype(f32).astype(bf16)
        count = mm(counts, spread)[0:1, :]
        start = mm(starts, spread)[0:1, :]
        target = jnp.where((slot_core == core) & (within < count), start + within, -1.0)
        hot[which] = (frame_rows == target).astype(f32).astype(bf16)

    def settle(j):
        for copy in spread_out(j):
            copy.wait_recv()
        keep(j).wait()
        pass_on(j).start()

    waiting = [0]
    for j in order:
        far(j).wait_recv()
        keep(j).start()
        for copy in spread_out(j):
            copy.start()
        waiting.append(j)
        if len(waiting) > 3:
            settle(waiting.pop(0))
    for j in waiting:
        settle(j)
    for j in [0] + order:
        pass_on(j).wait_recv()
    frame_ref[...] = (
        mm(hot[0], arr[...].reshape(slots, PART)) + mm(hot[1], par[...].reshape(slots, PART))
    ).astype(bf16)

    low, high = pl.ds(0, F // 2), pl.ds(F // 2, F // 2)
    up, down_by = {"head": peer(1)}, {"head": peer(3)}

    def gather_copy(i, src, slot, rows, where):
        return remote(src, gath.at[slot, rows, :], ag_send.at[i], ag_recv.at[i], where)

    gathers = [
        gather_copy(0, frame_ref.at[low, :], me, low, up),
        gather_copy(1, frame_ref.at[high, :], me, high, up),
        gather_copy(2, frame_ref.at[high, :], me, high, down_by),
        gather_copy(3, frame_ref.at[low, :], me, low, down_by),
        gather_copy(4, gath.at[peer(3), low, :], peer(3), low, up),
        gather_copy(5, gath.at[peer(1), high, :], peer(1), high, down_by),
    ]
    for i in (0, 2, 1, 3):
        gathers[i].start()
    gath[me] = frame_ref[...]
    gathers[0].wait_recv()
    gathers[4].start()
    gathers[2].wait_recv()
    gathers[5].start()
    for i in (1, 3, 4, 5):
        gathers[i].wait_recv()

    def norm_rows(r, carry):
        rows = pl.ds(pl.multiple_of(r * 32, 32), 32)
        xs = [gath[h, rows, :].astype(f32) for h in range(HEADS_ALL)]
        total = sum(jnp.sum(x, axis=1, keepdims=True) for x in xs)
        mean = total * (1.0 / (HEADS_ALL * PART))
        xs = [x - mean for x in xs]
        square = sum(jnp.sum(x * x, axis=1, keepdims=True) for x in xs)
        inv = lax.rsqrt(square * (1.0 / (HEADS_ALL * PART)) + EPSILON)
        inv_ref[rows, :] = jnp.broadcast_to(inv, (32, LANES))
        for h in range(HEADS_ALL):
            u = xs[h] * inv
            unit[h, rows, :] = u
            normed[rows, h * PART : (h + 1) * PART] = (u * gain_ref[h]).astype(bf16)
        return carry

    lax.fori_loop(0, F // 32, norm_rows, 0)

    halos = []
    for which, weight in ((0, wk), (1, wv)):
        loads[which].wait()
        rows = mm(normed[...], weight[...]).astype(bf16)
        for g in range(GROUPS):
            kv[1, which, g] = rows[:, g * LANES : (g + 1) * LANES]
        halos.append(
            remote(kv.at[1, which], kv.at[2, which], kv_send.at[which, 0], kv_recv.at[which, 0], {"seq": left})
        )
        halos.append(
            remote(kv.at[1, which], kv.at[0, which], kv_send.at[which, 1], kv_recv.at[which, 1], {"seq": right})
        )
        halos[-2].start()
        halos[-1].start()
    loads[2].wait()
    rows = mm(normed[...], wq[...]).astype(bf16)
    for g in range(GROUPS):
        qs[g] = rows[:, g * LANES : (g + 1) * LANES]

    def own_scores(g, carry):
        for sub in range(2):
            wts[2 * g + sub, 1] = mm_nt(qs[g] * mb[sub], kv[1, 0, g]) * scale + bias[1]
        return carry

    lax.fori_loop(0, GROUPS, own_scores, 0)
    for copy in halos:
        copy.wait_recv()

    def attend(g, carry):
        parts = []
        for sub in range(2):
            qm = qs[g] * mb[sub]
            score = [
                mm_nt(qm, kv[0, 0, g]) * scale + bias[0],
                wts[2 * g + sub, 1],
                mm_nt(qm, kv[2, 0, g]) * scale + bias[2],
            ]
            top = jnp.maximum(jnp.maximum(score[0], score[1]), score[2])
            top = jnp.max(top, axis=1, keepdims=True)
            lifted = [jnp.exp(x - top) for x in score]
            total = jnp.sum(lifted[0] + lifted[1] + lifted[2], axis=1, keepdims=True)
            inv = 1.0 / total
            acc = None
            for b in range(3):
                w = lifted[b] * inv
                wts[2 * g + sub, b] = w
                low = w.astype(bf16)
                wlow[2 * g + sub, b] = low
                term = mm(low, kv[b, 1, g])
                acc = term if acc is None else acc + term
            parts.append(acc * mf[sub])
        both = parts[0] + parts[1]
        att[g] = both
        columns = pl.ds(pl.multiple_of(g * LANES, LANES), LANES)
        res = (frame_ref[:, columns].astype(f32) + both).astype(bf16)
        res_low[g] = res
        res_ext[g, PAD : PAD + F, :] = res.astype(f32)
        return carry

    lax.fori_loop(0, GROUPS, attend, 0)

    def edges(low, halo, send, recv):
        return [
            remote(low.at[:, 0:PAD, :], halo.at[1], send.at[0], recv.at[0], {"seq": left}),
            remote(low.at[:, F - PAD : F, :], halo.at[0], send.at[1], recv.at[1], {"seq": right}),
        ]

    def place(halo, ext):
        for g in range(GROUPS):
            ext[g, 0:PAD, :] = halo[0, g].astype(f32)
            ext[g, PAD + F : 2 * PAD + F, :] = halo[1, g].astype(f32)

    res_edges = edges(res_low, res_halo, rh_send, rh_recv)
    for copy in res_edges:
        copy.start()

    def taps(ext, g, r, mirrored):
        base = seg_col[WIN + r : WIN + r + CHUNK, :]
        acc = jnp.zeros((CHUNK, LANES), f32)
        for t in range(KS):
            shift = (HALF_K - t) if mirrored else (t - HALF_K)
            same = seg_col[WIN + r + shift : WIN + r + shift + CHUNK, :] == base
            term = ext[g, PAD + r + shift : PAD + r + shift + CHUNK, :] * cw_ref[t : t + 1, pl.ds(pl.multiple_of(g * LANES, LANES), LANES)]
            acc = acc + jnp.where(same, term, 0.0)
        return acc

    def forward_conv(starts):
        def body(g, carry):
            columns = pl.ds(pl.multiple_of(g * LANES, LANES), LANES)
            for r in starts:
                conv = taps(res_ext, g, r, False)
                gate = lax.logistic(conv)
                out_ref[r : r + CHUNK, columns] = (
                    res_ext[g, PAD + r : PAD + r + CHUNK, :] + conv * gate
                ).astype(bf16)
                up = cot_ref[r : r + CHUNK, columns].astype(f32)
                gc = (up * gate * (1.0 + conv * (1.0 - gate))).astype(bf16)
                gc_low[g, r : r + CHUNK, :] = gc
                gc_ext[g, PAD + r : PAD + r + CHUNK, :] = gc.astype(f32)
            return carry

        lax.fori_loop(0, GROUPS, body, 0)

    def backward_conv(starts):
        def body(g, carry):
            columns = pl.ds(pl.multiple_of(g * LANES, LANES), LANES)
            for r in starts:
                moved = taps(gc_ext, g, r, True)
                up = cot_ref[r : r + CHUNK, columns].astype(f32)
                gres[g, r : r + CHUNK, :] = (up + moved).astype(bf16)
            return carry

        lax.fori_loop(0, GROUPS, body, 0)

    inner = (CHUNK, 2 * CHUNK)
    outer = (0, 3 * CHUNK)
    forward_conv(inner)
    for copy in res_edges:
        copy.wait_recv()
    place(res_halo, res_ext)
    forward_conv(outer)
    gc_edges = edges(gc_low, gc_halo, gh_send, gh_recv)
    for copy in gc_edges:
        copy.start()
    backward_conv(inner)
    for copy in gc_edges:
        copy.wait_recv()
    place(gc_halo, gc_ext)
    backward_conv(outer)

    def kv_grad_copies(g):
        return [
            remote(dsend.at[0, g], drecv.at[1, g], d_send.at[0, g], d_recv.at[1, g], {"seq": left}),
            remote(dsend.at[1, g], drecv.at[0, g], d_send.at[1, g], d_recv.at[0, g], {"seq": right}),
        ]

    def attend_back(g, carry):
        gq = []
        dk = [None, None, None]
        dv = [None, None, None]
        for sub in range(2):
            gm = gres[g] * mb[sub]
            qm = qs[g] * mb[sub]
            delta = jnp.sum(gm.astype(f32) * att[g], axis=1, keepdims=True)
            acc = None
            for b in range(3):
                gw = mm_nt(gm, kv[b, 1, g])
                ds = (wts[2 * g + sub, b] * (gw - delta) * scale).astype(bf16)
                term = mm(ds, kv[b, 0, g])
                acc = term if acc is None else acc + term
                dkt = mm_tn(ds, qm)
                dvt = mm_tn(wlow[2 * g + sub, b], gm)
                dk[b] = dkt if dk[b] is None else dk[b] + dkt
                dv[b] = dvt if dv[b] is None else dv[b] + dvt
            gq.append(acc * mf[sub])
        columns = pl.ds(pl.multiple_of(g * LANES, LANES), LANES)
        dq_ref[:, columns] = (gq[0] + gq[1]).astype(bf16)
        for slot, b in ((0, 0), (1, 2)):
            dsend[slot, g, 0] = dk[b].astype(bf16)
            dsend[slot, g, 1] = dv[b].astype(bf16)
        down[g, 0] = dk[1]
        down[g, 1] = dv[1]
        for copy in kv_grad_copies(g):
            copy.start()
        return carry

    lax.fori_loop(0, GROUPS, attend_back, 0)

    def weight_rows(ref, off):
        return ref[pl.ds(pl.multiple_of(peer(off) * PART, PART), PART), :]

    for off in (2, 1, 3, 0):
        pacc[off] = mm_nt(dq_ref[...], weight_rows(wq, off))

    for g in range(GROUPS):
        for copy in kv_grad_copies(g):
            copy.wait_recv()
        for which, dst in ((0, dkb), (1, dvb)):
            dst[:, g * LANES : (g + 1) * LANES] = (
                down[g, which] + drecv[0, g, which].astype(f32) + drecv[1, g, which].astype(f32)
            ).astype(bf16)

    row_sum = jnp.zeros((F, 1), f32)
    row_dot = jnp.zeros((F, 1), f32)
    exchanges = [
        remote(src.at[rows, :], dst.at[rows, :], p_send.at[i], p_recv.at[i], where)
        for i, (src, dst, rows, where) in enumerate((
            (psend.at[0], relay, low, up),
            (psend.at[0], relay, high, down_by),
            (psend.at[1], precv.at[0], high, up),
            (psend.at[2], precv.at[1], low, down_by),
            (psend.at[1], precv.at[0], low, up),
            (psend.at[2], precv.at[1], high, down_by),
        ))
    ]
    for off in (2, 1, 3, 0):
        part = pacc[off] + mm_nt(dkb[...], weight_rows(wk, off)) + mm_nt(dvb[...], weight_rows(wv, off))
        part = part * gain_ref[peer(off)]
        row_sum = row_sum + jnp.sum(part, axis=1, keepdims=True)
        row_dot = row_dot + jnp.sum(part * unit[peer(off)], axis=1, keepdims=True)
        if off == 2:
            psend[0] = part.astype(bf16)
            exchanges[0].start()
            exchanges[1].start()
        elif off == 1:
            pacc[1] = part
            psend[1, high, :] = part[F // 2 :, :].astype(bf16)
            exchanges[2].start()
        elif off == 3:
            pacc[3] = part
            psend[2, low, :] = part[: F // 2, :].astype(bf16)
            exchanges[3].start()
        else:
            pacc[0] = part

    lanes = lax.broadcasted_iota(jnp.int32, (F, LANES), 1)
    packed = jnp.where(lanes == 0, row_sum, jnp.where(lanes == 1, row_dot, 0.0))
    ssend[...] = jnp.transpose(packed)[0:8, :]
    exchanges[0].wait_recv()
    psend[1, low, :] = (pacc[1, low, :] + relay[low, :].astype(f32)).astype(bf16)
    exchanges[4].start()
    exchanges[1].wait_recv()
    psend[2, high, :] = (pacc[3, high, :] + relay[high, :].astype(f32)).astype(bf16)
    exchanges[5].start()
    shared = [
        remote(ssend, srecv.at[off - 1], s_send.at[off - 1], s_recv.at[off - 1], {"head": peer(off)})
        for off in (2, 1, 3)
    ]
    for copy in shared:
        copy.start()
    for copy in exchanges[2:] + shared:
        copy.wait_recv()
    sums = ssend[...] + srecv[0] + srecv[1] + srecv[2]
    sums = jnp.transpose(jnp.concatenate([sums] * (LANES // 8), axis=0)) * (1.0 / (HEADS_ALL * PART))
    inv_ref[:, 1:2] = sums[:, 0:1]
    inv_ref[:, 2:3] = sums[:, 1:2]

    def finish(r, carry):
        rows = pl.ds(pl.multiple_of(r * 32, 32), 32)
        scaled = pacc[0, rows, :]
        for i in range(2):
            scaled = scaled + precv[i, rows, :].astype(f32)
        through = inv_ref[rows, 0:1] * (
            scaled - inv_ref[rows, 1:2] - unit[me, rows, :] * inv_ref[rows, 2:3]
        )
        for g in range(GROUPS):
            columns = slice(g * LANES, (g + 1) * LANES)
            grad_ref[rows, columns] = (gres[g, rows, :].astype(f32) + through[:, columns]).astype(bf16)
        return carry

    lax.fori_loop(0, F // 32, finish, 0)

    for j in [0] + order:
        if j:
            far(j).wait_send()
        pass_on(j).wait_send()
        for copy in spread_out(j):
            copy.wait_send()
    for copy in gathers + halos + res_edges + gc_edges + exchanges + shared:
        copy.wait_send()
    for g in range(GROUPS):
        for copy in kv_grad_copies(g):
            copy.wait_send()


def block_call(loader_rows, plan, lengths, gain, wq, wk, wv, conv_weight, cotangent):
    f32, bf16 = jnp.float32, jnp.bfloat16
    seq_count = lax.axis_size("seq")
    span = F + 2 * WIN
    pairs = seq_count // 2
    tile = loader_rows.shape[0] // pairs
    slots = pairs * tile
    wide = 4 if pairs > 8 else 2
    deep = pairs // wide
    loader = loader_rows.reshape(deep, wide, tile, PART)
    vmem = pl.BlockSpec(memory_space=pltpu.VMEM)
    hbm = pl.BlockSpec(memory_space=pl.ANY)
    v = pltpu.VMEM
    dma = pltpu.SemaphoreType.DMA
    shape = jax.ShapeDtypeStruct((F, PART), bf16)
    return pl.pallas_call(
        block_kernel,
        out_shape=(shape, shape),
        in_specs=[vmem] * 5 + [hbm] * 4,
        out_specs=(vmem, vmem),
        scratch_shapes=[
            v((deep, wide, tile, PART), bf16),
            v((deep, wide, tile, PART), bf16),
            v((deep, wide, tile, PART), bf16),
            v((2, F, slots), bf16),
            v((8, F), f32),
            v((8, span), f32),
            v((span, LANES), f32),
            v((HEADS_ALL, 1, PART), f32),
            v((F, PART), bf16),
            v((HEADS_ALL, F, PART), bf16),
            v((HEADS_ALL, F, PART), f32),
            v((F, HEADS_ALL * PART), bf16),
            v((F, LANES), f32),
            v((HEADS_ALL * PART, PART), bf16),
            v((HEADS_ALL * PART, PART), bf16),
            v((HEADS_ALL * PART, PART), bf16),
            v((3, 2, GROUPS, F, LANES), bf16),
            v((GROUPS, F, LANES), bf16),
            v((3, F, F), f32),
            v((2 * GROUPS, 3, F, F), f32),
            v((2 * GROUPS, 3, F, F), bf16),
            v((GROUPS, F, LANES), f32),
            v((GROUPS, F, LANES), bf16),
            v((GROUPS, F + 2 * PAD, LANES), f32),
            v((2, GROUPS, PAD, LANES), bf16),
            v((GROUPS, F, LANES), bf16),
            v((GROUPS, F + 2 * PAD, LANES), f32),
            v((2, GROUPS, PAD, LANES), bf16),
            v((GROUPS, F, LANES), bf16),
            v((F, PART), bf16),
            v((2, GROUPS, 2, F, LANES), bf16),
            v((2, GROUPS, 2, F, LANES), bf16),
            v((GROUPS, 2, F, LANES), f32),
            v((F, PART), bf16),
            v((F, PART), bf16),
            v((HEADS_ALL, F, PART), f32),
            v((3, F, PART), bf16),
            v((F, PART), bf16),
            v((2, F, PART), bf16),
            v((8, F), f32),
            v((3, 8, F), f32),
            dma((deep,)),
            dma((deep,)),
            dma((deep, wide)),
            dma((deep, wide)),
            dma((deep,)),
            dma((deep,)),
            dma((deep,)),
            dma((1,)),
            dma((3,)),
            dma((6,)),
            dma((6,)),
            dma((2, 2)),
            dma((2, 2)),
            dma((2,)),
            dma((2,)),
            dma((2,)),
            dma((2,)),
            dma((2, GROUPS)),
            dma((2, GROUPS)),
            dma((6,)),
            dma((6,)),
            dma((3,)),
            dma((3,)),
        ],
        compiler_params=pltpu.CompilerParams(
            collective_id=0, has_side_effects=True, vmem_limit_bytes=56 * 1024 * 1024
        ),
    )(plan, lengths[None, :], gain[None, :], conv_weight, cotangent, loader, wq, wk, wv)


def on_device(loader_rows, plan, lengths, gain, wq, wk, wv, conv_weight, cotangent):
    return block_call(loader_rows, plan, lengths, gain, wq, wk, wv, conv_weight, cotangent)


def solution(mesh):
    placed = (
        P("seq", "head"),
        P(),
        P(),
        P(),
        P(None, "head"),
        P(None, "head"),
        P(None, "head"),
        P(None, "head"),
        P("seq", "head"),
    )
    return jax.shard_map(
        on_device,
        mesh=mesh,
        in_specs=placed,
        out_specs=(P("seq", "head"), P("seq", "head")),
        check_vma=False,
    )
```

```python
import math

import jax
import jax.numpy as jnp
from jax import lax
from jax.experimental import pallas as pl
from jax.experimental.pallas import tpu as pltpu
from jax.sharding import PartitionSpec as P

HEAD_DIM = 64
KS = 31
HALF_K = 15
WIN = 256
F = 256
PART = 384
GROUPS = 3
LANES = 128
HEADS_ALL = 4
CHUNK = 64
PAD = 16


EPSILON = 1e-05
MESH = pl.DeviceIdType.MESH


def mm(a, b):
    return jnp.dot(a, b, preferred_element_type=jnp.float32)


def mm_nt(a, b):
    return lax.dot_general(a, b, (((1,), (1,)), ((), ())), preferred_element_type=jnp.float32)


def mm_tn(a, b):
    return lax.dot_general(a, b, (((0,), (0,)), ((), ())), preferred_element_type=jnp.float32)


def block_kernel(
    plan_ref, len_ref, gain_all, cw_ref, cot_ref, loader, wq_hbm, wk_hbm, wv_hbm,
    out_ref, grad_ref,
    xin, arr, par, hot, len_row, seg_row, seg_col, gain_ref, frame_ref, gath, unit, normed, inv_ref, wq, wk, wv, kv, qs, bias, wts, wlow, att,
    res_low, res_ext, res_halo, gc_low, gc_ext, gc_halo, gres,
    dq_ref, dsend, drecv, down, dkb, dvb, pacc, psend, precv, ssend, srecv,
    z_send, z_recv, x_send, x_recv, l_sem, f_send, f_recv, w_sem, ag_send, ag_recv, kv_send, kv_recv, rh_send, rh_recv, gh_send, gh_recv,
    d_send, d_recv, p_send, p_recv, s_send, s_recv,
):
    seq_count = lax.axis_size("seq")
    me = lax.axis_index("head")
    seq = lax.axis_index("seq")
    right = lax.rem(seq + 1, seq_count)
    left = lax.rem(seq + seq_count - 1, seq_count)
    scale = 1.0 / math.sqrt(HEAD_DIM)
    f32, bf16 = jnp.float32, jnp.bfloat16

    def peer(off):
        return lax.rem(me + off, HEADS_ALL)

    def remote(src, dst, send, recv, where):
        return pltpu.make_async_remote_copy(
            src_ref=src, dst_ref=dst, send_sem=send, recv_sem=recv, device_id=where, device_id_type=MESH
        )

    loads = [
        pltpu.make_async_copy(src, dst, w_sem.at[i])
        for i, (src, dst) in enumerate(((wk_hbm, wk), (wv_hbm, wv), (wq_hbm, wq)))
    ]
    for copy in loads:
        copy.start()

    deep, wide, tile = loader.shape[0], loader.shape[1], loader.shape[2]
    slots, capacity = deep * wide * tile, tile // 2
    core = lax.rem(seq, 2)
    pair = lax.div(seq, 2)
    z, x = lax.div(pair, wide), lax.rem(pair, wide)
    partner = seq + 1 - 2 * core
    half = deep // 2
    steps = sorted(range(1, wide), key=lambda k: min(k, wide - k))

    def at_z(j):
        return (lax.rem(z + j, deep) * wide + x) * 2 + core

    def at_x(k):
        return (z * wide + lax.rem(x + k, wide)) * 2 + core

    barrier = pltpu.get_barrier_semaphore()

    def both_ways(act):
        act(half)

        def body(i, carry):
            act(half - i)
            act(half + i)
            return carry

        lax.fori_loop(1, half, body, 0)

    both_ways(
        lambda j: pl.semaphore_signal(barrier, inc=1, device_id={"seq": at_z(j)}, device_id_type=MESH)
    )
    for k in range(1, wide):
        pl.semaphore_signal(barrier, inc=1, device_id={"seq": at_x(k)}, device_id_type=MESH)
    for off in (1, 2, 3):
        pl.semaphore_signal(barrier, inc=1, device_id={"head": peer(off)}, device_id_type=MESH)
    for side in (left, right, partner):
        pl.semaphore_signal(barrier, inc=1, device_id={"seq": side}, device_id_type=MESH)

    for h in range(HEADS_ALL):
        gain_ref[h] = gain_all[h * PART : (h + 1) * PART][None, :]
    len_row[...] = jnp.zeros_like(len_row)
    len_row[0:1, 0 : len_ref.shape[1]] = len_ref[...].astype(f32)
    rows_i = lax.broadcasted_iota(jnp.int32, (F, F), 0)
    cols_i = lax.broadcasted_iota(jnp.int32, (F, F), 1)
    pl.semaphore_wait(barrier, deep + wide + 4)

    def across(k):
        return remote(
            loader.at[:, lax.rem(x + k, wide)], xin.at[x], x_send.at[k], x_recv.at[k], {"seq": at_x(k)}
        )

    def held(k, layer):
        came = lax.rem(x + wide - k, wide)
        return xin.at[came, layer] if k else loader.at[layer, x]

    def far(j, k):
        came = lax.rem(x + wide - k, wide)
        return remote(
            held(k, lax.rem(z + j, deep)), arr.at[z, came],
            z_send.at[k, j], z_recv.at[k, j], {"seq": at_z(j)},
        )

    def keep(k):
        return pltpu.make_async_copy(held(k, z), arr.at[z, lax.rem(x + wide - k, wide)], l_sem.at[k])

    def pass_on(j, k):
        layer, came = lax.rem(z + deep - j, deep), lax.rem(x + wide - k, wide)
        return remote(
            arr.at[layer, came], par.at[layer, came], f_send.at[k, j], f_recv.at[k, j], {"seq": partner}
        )

    for k in steps[::-1]:
        across(k).start()
    both_ways(lambda j: far(j, 0).start())
    keep(0).start()
    for k in steps:
        across(k).wait_recv()
        both_ways(lambda j: far(j, k).start())
        keep(k).start()

    lens = len_row[0:1, :]
    ends_col = jnp.sum(jnp.where(cols_i <= rows_i, lens, 0.0), axis=1, keepdims=True)
    lens_col = jnp.transpose(jnp.broadcast_to(lens, (LANES, F)))[:, 0:1]
    ends_row = jnp.sum(jnp.where(rows_i <= cols_i, lens_col, 0.0), axis=0, keepdims=True)
    total = (seq_count * F) * 1.0
    first = (seq * F - WIN).astype(f32)
    for b in range(3):
        place_row = lax.broadcasted_iota(jnp.int32, (1, F), 1).astype(f32) + (first + b * F)
        inside = (place_row >= 0.0) & (place_row < total)
        count = jnp.sum((ends_col <= place_row).astype(f32), axis=0, keepdims=True)
        seg_row[0:1, b * F : (b + 1) * F] = jnp.where(inside, count, -1.0)
        place_col = lax.broadcasted_iota(jnp.int32, (F, 1), 0).astype(f32) + (first + b * F)
        inside = (place_col >= 0.0) & (place_col < total)
        count = jnp.sum((ends_row <= place_col).astype(f32), axis=1, keepdims=True)
        seg_col[b * F : (b + 1) * F, :] = jnp.broadcast_to(jnp.where(inside, count, -1.0), (F, LANES))

    own_seg = seg_col[WIN : WIN + F, 0:1]
    for b in range(3):
        ok = seg_row[0:1, b * F : (b + 1) * F] == own_seg
        if b == 0:
            ok = ok & (cols_i >= rows_i)
        if b == 2:
            ok = ok & (cols_i < rows_i)
        bias[b] = jnp.where(ok, 0.0, -jnp.inf)

    lane = lax.broadcasted_iota(jnp.int32, (1, LANES), 1)
    mf = [(lane < HEAD_DIM).astype(f32), (lane >= HEAD_DIM).astype(f32)]
    mb = [m.astype(bf16) for m in mf]

    chosen = (lax.broadcasted_iota(jnp.int32, (8, seq_count), 1) == seq).astype(f32).astype(bf16)
    counts = mm_nt(chosen, plan_ref[...].astype(f32).astype(bf16)).astype(bf16)
    lower = lax.broadcasted_iota(jnp.int32, (seq_count, seq_count), 0)
    upper = lax.broadcasted_iota(jnp.int32, (seq_count, seq_count), 1)
    starts = mm(counts, (lower < upper).astype(f32).astype(bf16)).astype(bf16)
    loader_row = lax.broadcasted_iota(jnp.int32, (seq_count, slots), 0)
    slot_pair = lax.shift_right_logical(
        lax.broadcasted_iota(jnp.int32, (seq_count, slots), 1), jnp.int32(tile.bit_length() - 1)
    )
    slot_row = lax.broadcasted_iota(jnp.int32, (1, slots), 1)
    slot_core = lax.shift_right_logical(slot_row, jnp.int32(capacity.bit_length() - 1)) & 1
    within = (slot_row & (capacity - 1)).astype(f32)
    frame_rows = lax.broadcasted_iota(jnp.int32, (F, slots), 0).astype(f32)
    for which, parity in ((0, core), (1, 1 - core)):
        spread = (loader_row == 2 * slot_pair + parity).astype(f32).astype(bf16)
        count = mm(counts, spread)[0:1, :]
        start = mm(starts, spread)[0:1, :]
        target = jnp.where((slot_core == core) & (within < count), start + within, -1.0)
        hot[which] = (frame_rows == target).astype(f32).astype(bf16)

    for k in [0] + steps:
        keep(k).wait()
        pass_on(0, k).start()

        def land(j):
            far(j, k).wait_recv()
            pass_on(j, k).start()

        both_ways(land)
    for k in [0] + steps:
        pass_on(0, k).wait_recv()
        both_ways(lambda j: pass_on(j, k).wait_recv())
    frame_ref[...] = (
        mm(hot[0], arr[...].reshape(slots, PART)) + mm(hot[1], par[...].reshape(slots, PART))
    ).astype(bf16)

    low, high = pl.ds(0, F // 2), pl.ds(F // 2, F // 2)
    up, down_by = {"head": peer(1)}, {"head": peer(3)}

    def gather_copy(i, src, slot, rows, where):
        return remote(src, gath.at[slot, rows, :], ag_send.at[i], ag_recv.at[i], where)

    gathers = [
        gather_copy(0, frame_ref.at[low, :], me, low, up),
        gather_copy(1, frame_ref.at[high, :], me, high, up),
        gather_copy(2, frame_ref.at[high, :], me, high, down_by),
        gather_copy(3, frame_ref.at[low, :], me, low, down_by),
        gather_copy(4, gath.at[peer(3), low, :], peer(3), low, up),
        gather_copy(5, gath.at[peer(1), high, :], peer(1), high, down_by),
    ]
    for i in (0, 2, 1, 3):
        gathers[i].start()
    gath[me] = frame_ref[...]
    gathers[0].wait_recv()
    gathers[4].start()
    gathers[2].wait_recv()
    gathers[5].start()
    for i in (1, 3, 4, 5):
        gathers[i].wait_recv()

    def norm_rows(r, carry):
        rows = pl.ds(pl.multiple_of(r * 32, 32), 32)
        xs = [gath[h, rows, :].astype(f32) for h in range(HEADS_ALL)]
        total = sum(jnp.sum(x, axis=1, keepdims=True) for x in xs)
        mean = total * (1.0 / (HEADS_ALL * PART))
        xs = [x - mean for x in xs]
        square = sum(jnp.sum(x * x, axis=1, keepdims=True) for x in xs)
        inv = lax.rsqrt(square * (1.0 / (HEADS_ALL * PART)) + EPSILON)
        inv_ref[rows, :] = jnp.broadcast_to(inv, (32, LANES))
        for h in range(HEADS_ALL):
            u = xs[h] * inv
            unit[h, rows, :] = u
            normed[rows, h * PART : (h + 1) * PART] = (u * gain_ref[h]).astype(bf16)
        return carry

    lax.fori_loop(0, F // 32, norm_rows, 0)

    halos = []
    for which, weight in ((0, wk), (1, wv)):
        loads[which].wait()
        rows = mm(normed[...], weight[...]).astype(bf16)
        for g in range(GROUPS):
            kv[1, which, g] = rows[:, g * LANES : (g + 1) * LANES]
        halos.append(
            remote(kv.at[1, which], kv.at[2, which], kv_send.at[which, 0], kv_recv.at[which, 0], {"seq": left})
        )
        halos.append(
            remote(kv.at[1, which], kv.at[0, which], kv_send.at[which, 1], kv_recv.at[which, 1], {"seq": right})
        )
        halos[-2].start()
        halos[-1].start()
    loads[2].wait()
    rows = mm(normed[...], wq[...]).astype(bf16)
    for g in range(GROUPS):
        qs[g] = rows[:, g * LANES : (g + 1) * LANES]

    def own_scores(g, carry):
        for sub in range(2):
            wts[2 * g + sub, 1] = mm_nt(qs[g] * mb[sub], kv[1, 0, g]) * scale + bias[1]
        return carry

    lax.fori_loop(0, GROUPS, own_scores, 0)
    for copy in halos[:2]:
        copy.wait_recv()

    def weigh(g, carry):
        for sub in range(2):
            qm = qs[g] * mb[sub]
            score = [
                mm_nt(qm, kv[0, 0, g]) * scale + bias[0],
                wts[2 * g + sub, 1],
                mm_nt(qm, kv[2, 0, g]) * scale + bias[2],
            ]
            top = jnp.maximum(jnp.maximum(score[0], score[1]), score[2])
            top = jnp.max(top, axis=1, keepdims=True)
            lifted = [jnp.exp(x - top) for x in score]
            total = jnp.sum(lifted[0] + lifted[1] + lifted[2], axis=1, keepdims=True)
            inv = 1.0 / total
            for b in range(3):
                w = lifted[b] * inv
                wts[2 * g + sub, b] = w
                wlow[2 * g + sub, b] = w.astype(bf16)
        return carry

    lax.fori_loop(0, GROUPS, weigh, 0)
    for copy in halos[2:]:
        copy.wait_recv()

    def attend(g, carry):
        parts = []
        for sub in range(2):
            acc = mm(wlow[2 * g + sub, 0], kv[0, 1, g])
            for b in (1, 2):
                acc = acc + mm(wlow[2 * g + sub, b], kv[b, 1, g])
            parts.append(acc * mf[sub])
        both = parts[0] + parts[1]
        att[g] = both
        columns = pl.ds(pl.multiple_of(g * LANES, LANES), LANES)
        res = (frame_ref[:, columns].astype(f32) + both).astype(bf16)
        res_low[g] = res
        res_ext[g, PAD : PAD + F, :] = res.astype(f32)
        return carry

    lax.fori_loop(0, GROUPS, attend, 0)

    def edges(low, halo, send, recv):
        return [
            remote(low.at[:, 0:PAD, :], halo.at[1], send.at[0], recv.at[0], {"seq": left}),
            remote(low.at[:, F - PAD : F, :], halo.at[0], send.at[1], recv.at[1], {"seq": right}),
        ]

    def place(halo, ext):
        for g in range(GROUPS):
            ext[g, 0:PAD, :] = halo[0, g].astype(f32)
            ext[g, PAD + F : 2 * PAD + F, :] = halo[1, g].astype(f32)

    res_edges = edges(res_low, res_halo, rh_send, rh_recv)
    for copy in res_edges:
        copy.start()

    def taps(ext, r, mirrored):
        base = seg_col[WIN + r : WIN + r + CHUNK, :]
        acc = [jnp.zeros((CHUNK, LANES), f32) for _ in range(GROUPS)]
        for t in range(KS):
            shift = (HALF_K - t) if mirrored else (t - HALF_K)
            same = seg_col[WIN + r + shift : WIN + r + shift + CHUNK, :] == base
            for g in range(GROUPS):
                term = ext[g, PAD + r + shift : PAD + r + shift + CHUNK, :]
                term = term * cw_ref[t : t + 1, g * LANES : (g + 1) * LANES]
                acc[g] = acc[g] + jnp.where(same, term, 0.0)
        return acc

    def forward_conv(starts):
        for r in starts:
            for g, conv in enumerate(taps(res_ext, r, False)):
                columns = slice(g * LANES, (g + 1) * LANES)
                gate = lax.logistic(conv)
                out_ref[r : r + CHUNK, columns] = (
                    res_ext[g, PAD + r : PAD + r + CHUNK, :] + conv * gate
                ).astype(bf16)
                up = cot_ref[r : r + CHUNK, columns].astype(f32)
                gc = (up * gate * (1.0 + conv * (1.0 - gate))).astype(bf16)
                gc_low[g, r : r + CHUNK, :] = gc
                gc_ext[g, PAD + r : PAD + r + CHUNK, :] = gc.astype(f32)

    def backward_conv(starts):
        for r in starts:
            for g, moved in enumerate(taps(gc_ext, r, True)):
                columns = slice(g * LANES, (g + 1) * LANES)
                up = cot_ref[r : r + CHUNK, columns].astype(f32)
                gres[g, r : r + CHUNK, :] = (up + moved).astype(bf16)

    inner = (CHUNK, 2 * CHUNK)
    outer = (0, 3 * CHUNK)
    forward_conv(inner)
    for copy in res_edges:
        copy.wait_recv()
    place(res_halo, res_ext)
    forward_conv(outer)
    gc_edges = edges(gc_low, gc_halo, gh_send, gh_recv)
    for copy in gc_edges:
        copy.start()
    backward_conv(inner)
    for copy in gc_edges:
        copy.wait_recv()
    place(gc_halo, gc_ext)
    backward_conv(outer)

    def kv_grad_copies(g):
        return [
            remote(dsend.at[0, g], drecv.at[1, g], d_send.at[0, g], d_recv.at[1, g], {"seq": left}),
            remote(dsend.at[1, g], drecv.at[0, g], d_send.at[1, g], d_recv.at[0, g], {"seq": right}),
        ]

    def attend_back(g, carry):
        gq = []
        dk = [None, None, None]
        dv = [None, None, None]
        for sub in range(2):
            gm = gres[g] * mb[sub]
            qm = qs[g] * mb[sub]
            delta = jnp.sum(gm.astype(f32) * att[g], axis=1, keepdims=True)
            acc = None
            for b in range(3):
                gw = mm_nt(gm, kv[b, 1, g])
                ds = (wts[2 * g + sub, b] * (gw - delta) * scale).astype(bf16)
                term = mm(ds, kv[b, 0, g])
                acc = term if acc is None else acc + term
                dkt = mm_tn(ds, qm)
                dvt = mm_tn(wlow[2 * g + sub, b], gm)
                dk[b] = dkt if dk[b] is None else dk[b] + dkt
                dv[b] = dvt if dv[b] is None else dv[b] + dvt
            gq.append(acc * mf[sub])
        columns = pl.ds(pl.multiple_of(g * LANES, LANES), LANES)
        dq_ref[:, columns] = (gq[0] + gq[1]).astype(bf16)
        for slot, b in ((0, 0), (1, 2)):
            dsend[slot, g, 0] = dk[b].astype(bf16)
            dsend[slot, g, 1] = dv[b].astype(bf16)
        down[g, 0] = dk[1]
        down[g, 1] = dv[1]
        for copy in kv_grad_copies(g):
            copy.start()
        return carry

    lax.fori_loop(0, GROUPS, attend_back, 0)

    def weight_rows(ref, off):
        return ref[pl.ds(pl.multiple_of(peer(off) * PART, PART), PART), :]

    for off in (2, 1, 3, 0):
        pacc[off] = mm_nt(dq_ref[...], weight_rows(wq, off))

    for g in range(GROUPS):
        for copy in kv_grad_copies(g):
            copy.wait_recv()
        for which, dst in ((0, dkb), (1, dvb)):
            dst[:, g * LANES : (g + 1) * LANES] = (
                down[g, which] + drecv[0, g, which].astype(f32) + drecv[1, g, which].astype(f32)
            ).astype(bf16)

    row_sum = jnp.zeros((F, 1), f32)
    row_dot = jnp.zeros((F, 1), f32)
    exchanges = []
    for off in (2, 1, 3, 0):
        part = pacc[off] + mm_nt(dkb[...], weight_rows(wk, off)) + mm_nt(dvb[...], weight_rows(wv, off))
        part = part * gain_ref[peer(off)]
        row_sum = row_sum + jnp.sum(part, axis=1, keepdims=True)
        row_dot = row_dot + jnp.sum(part * unit[peer(off)], axis=1, keepdims=True)
        if off:
            psend[off - 1] = part.astype(bf16)
            copy = remote(
                psend.at[off - 1], precv.at[off - 1], p_send.at[off - 1], p_recv.at[off - 1], {"head": peer(off)}
            )
            copy.start()
            exchanges.append(copy)
        else:
            pacc[0] = part

    lanes = lax.broadcasted_iota(jnp.int32, (F, LANES), 1)
    packed = jnp.where(lanes == 0, row_sum, jnp.where(lanes == 1, row_dot, 0.0))
    ssend[...] = jnp.transpose(packed)[0:8, :]
    for off in (2, 1, 3):
        copy = remote(ssend, srecv.at[off - 1], s_send.at[off - 1], s_recv.at[off - 1], {"head": peer(off)})
        copy.start()
        exchanges.append(copy)
    for copy in exchanges:
        copy.wait_recv()
    sums = ssend[...] + srecv[0] + srecv[1] + srecv[2]
    sums = jnp.transpose(jnp.concatenate([sums] * (LANES // 8), axis=0)) * (1.0 / (HEADS_ALL * PART))
    inv_ref[:, 1:2] = sums[:, 0:1]
    inv_ref[:, 2:3] = sums[:, 1:2]

    def finish(r, carry):
        rows = pl.ds(pl.multiple_of(r * 32, 32), 32)
        scaled = pacc[0, rows, :]
        for i in range(3):
            scaled = scaled + precv[i, rows, :].astype(f32)
        through = inv_ref[rows, 0:1] * (
            scaled - inv_ref[rows, 1:2] - unit[me, rows, :] * inv_ref[rows, 2:3]
        )
        for g in range(GROUPS):
            columns = slice(g * LANES, (g + 1) * LANES)
            grad_ref[rows, columns] = (gres[g, rows, :].astype(f32) + through[:, columns]).astype(bf16)
        return carry

    lax.fori_loop(0, F // 32, finish, 0)

    for k in [0] + steps:
        if k:
            across(k).wait_send()

        def drain(j):
            far(j, k).wait_send()
            pass_on(j, k).wait_send()

        both_ways(drain)
        pass_on(0, k).wait_send()
    for copy in gathers + halos + res_edges + gc_edges + exchanges:
        copy.wait_send()
    for g in range(GROUPS):
        for copy in kv_grad_copies(g):
            copy.wait_send()


def copy_kernel(a_ref, b_ref, c_ref, d_ref, held, came, gone):
    ins = [pltpu.make_async_copy(r, held.at[i], came.at[i]) for i, r in enumerate((a_ref, b_ref))]
    outs = [pltpu.make_async_copy(held.at[i], r, gone.at[i]) for i, r in enumerate((c_ref, d_ref))]
    for copy in ins:
        copy.start()
    for i in range(2):
        ins[i].wait()
        outs[i].start()
    for copy in outs:
        copy.wait()


def hand_out(results):
    hbm = pl.BlockSpec(memory_space=pl.ANY)
    shape = jax.ShapeDtypeStruct((F, PART), jnp.bfloat16)
    dma = pltpu.SemaphoreType.DMA
    return pl.pallas_call(
        copy_kernel,
        out_shape=(shape, shape),
        in_specs=[hbm, hbm],
        out_specs=(hbm, hbm),
        scratch_shapes=[pltpu.VMEM((2, F, PART), jnp.bfloat16), dma((2,)), dma((2,))],
    )(*results)


def block_call(loader_rows, plan, lengths, gain, wq, wk, wv, conv_weight, cotangent):
    f32, bf16 = jnp.float32, jnp.bfloat16
    seq_count = lax.axis_size("seq")
    span = F + 2 * WIN
    pairs = seq_count // 2
    tile = loader_rows.shape[0] // pairs
    slots = pairs * tile
    wide = 4 if pairs > 8 else 2
    deep = pairs // wide
    loader = loader_rows.reshape(deep, wide, tile, PART)
    vmem = pl.BlockSpec(memory_space=pltpu.VMEM)
    hbm = pl.BlockSpec(memory_space=pl.ANY)
    v = pltpu.VMEM
    dma = pltpu.SemaphoreType.DMA
    shape = jax.ShapeDtypeStruct((F, PART), bf16)
    return pl.pallas_call(
        block_kernel,
        out_shape=(shape, shape),
        in_specs=[vmem] * 5 + [hbm] * 4,
        out_specs=(vmem, vmem),
        scratch_shapes=[
            v((wide, deep, tile, PART), bf16),
            v((deep, wide, tile, PART), bf16),
            v((deep, wide, tile, PART), bf16),
            v((2, F, slots), bf16),
            v((8, F), f32),
            v((8, span), f32),
            v((span, LANES), f32),
            v((HEADS_ALL, 1, PART), f32),
            v((F, PART), bf16),
            v((HEADS_ALL, F, PART), bf16),
            v((HEADS_ALL, F, PART), f32),
            v((F, HEADS_ALL * PART), bf16),
            v((F, LANES), f32),
            v((HEADS_ALL * PART, PART), bf16),
            v((HEADS_ALL * PART, PART), bf16),
            v((HEADS_ALL * PART, PART), bf16),
            v((3, 2, GROUPS, F, LANES), bf16),
            v((GROUPS, F, LANES), bf16),
            v((3, F, F), f32),
            v((2 * GROUPS, 3, F, F), f32),
            v((2 * GROUPS, 3, F, F), bf16),
            v((GROUPS, F, LANES), f32),
            v((GROUPS, F, LANES), bf16),
            v((GROUPS, F + 2 * PAD, LANES), f32),
            v((2, GROUPS, PAD, LANES), bf16),
            v((GROUPS, F, LANES), bf16),
            v((GROUPS, F + 2 * PAD, LANES), f32),
            v((2, GROUPS, PAD, LANES), bf16),
            v((GROUPS, F, LANES), bf16),
            v((F, PART), bf16),
            v((2, GROUPS, 2, F, LANES), bf16),
            v((2, GROUPS, 2, F, LANES), bf16),
            v((GROUPS, 2, F, LANES), f32),
            v((F, PART), bf16),
            v((F, PART), bf16),
            v((HEADS_ALL, F, PART), f32),
            v((3, F, PART), bf16),
            v((3, F, PART), bf16),
            v((8, F), f32),
            v((3, 8, F), f32),
            dma((wide, deep)),
            dma((wide, deep)),
            dma((wide,)),
            dma((wide,)),
            dma((wide,)),
            dma((wide, deep)),
            dma((wide, deep)),
            dma((3,)),
            dma((6,)),
            dma((6,)),
            dma((2, 2)),
            dma((2, 2)),
            dma((2,)),
            dma((2,)),
            dma((2,)),
            dma((2,)),
            dma((2, GROUPS)),
            dma((2, GROUPS)),
            dma((3,)),
            dma((3,)),
            dma((3,)),
            dma((3,)),
        ],
        compiler_params=pltpu.CompilerParams(
            collective_id=0, has_side_effects=True, vmem_limit_bytes=56 * 1024 * 1024
        ),
    )(plan, lengths[None, :], gain, conv_weight, cotangent, loader, wq, wk, wv)


def on_device(loader_rows, plan, lengths, gain, wq, wk, wv, conv_weight, cotangent):
    return hand_out(block_call(loader_rows, plan, lengths, gain, wq, wk, wv, conv_weight, cotangent))


def solution(mesh):
    placed = (
        P("seq", "head"),
        P(),
        P(),
        P(),
        P(None, "head"),
        P(None, "head"),
        P(None, "head"),
        P(None, "head"),
        P("seq", "head"),
    )
    return jax.shard_map(
        on_device,
        mesh=mesh,
        in_specs=placed,
        out_specs=(P("seq", "head"), P("seq", "head")),
        check_vma=False,
    )
```

```python
import math

import jax
import jax.numpy as jnp
from jax import lax
from jax.experimental import pallas as pl
from jax.experimental.pallas import tpu as pltpu
from jax.sharding import PartitionSpec as P

HEAD_DIM = 64
KS = 31
HALF_K = 15
WIN = 256
F = 256
PART = 384
GROUPS = 3
LANES = 128
HEADS_ALL = 4
CHUNK = 64
PAD = 16


EPSILON = 1e-05
MESH = pl.DeviceIdType.MESH


def mm(a, b):
    return jnp.dot(a, b, preferred_element_type=jnp.float32)


def mm_nt(a, b):
    return lax.dot_general(a, b, (((1,), (1,)), ((), ())), preferred_element_type=jnp.float32)


def block_kernel(
    plan_ref, len_ref, gain_all, cw_ref, cot_ref, loader, wq_hbm, wk_hbm, wv_hbm,
    out_ref, grad_ref,
    xin, arr, par, hot, len_row, seg_row, seg_col, gain_ref, frame_ref, gath, unit, normed, inv_ref, wq, wk, wv, kv, qs, bias, wts, wlow, att,
    res_low, res_ext, res_halo, gc_low, gc_ext, gc_halo, gres,
    dq_ref, dq_part, dsend, drecv, down, dkb, dvb, pacc, psend, precv, ssend, srecv,
    z_send, z_recv, x_send, x_recv, l_sem, f_send, f_recv, w_sem, ag_send, ag_recv, kv_send, kv_recv, rh_send, rh_recv, gh_send, gh_recv,
    d_send, d_recv, p_send, p_recv, s_send, s_recv,
):
    seq_count = lax.axis_size("seq")
    me = lax.axis_index("head")
    seq = lax.axis_index("seq")
    right = lax.rem(seq + 1, seq_count)
    left = lax.rem(seq + seq_count - 1, seq_count)
    scale = 1.0 / math.sqrt(HEAD_DIM)
    f32, bf16 = jnp.float32, jnp.bfloat16

    def peer(off):
        return lax.rem(me + off, HEADS_ALL)

    def remote(src, dst, send, recv, where):
        return pltpu.make_async_remote_copy(
            src_ref=src, dst_ref=dst, send_sem=send, recv_sem=recv, device_id=where, device_id_type=MESH
        )

    loads = [
        pltpu.make_async_copy(src, dst, w_sem.at[i])
        for i, (src, dst) in enumerate(((wk_hbm, wk), (wv_hbm, wv), (wq_hbm, wq)))
    ]
    for copy in loads:
        copy.start()

    deep, wide, tile = loader.shape[0], loader.shape[1], loader.shape[2]
    slots, capacity = deep * wide * tile, tile // 2
    core = lax.rem(seq, 2)
    pair = lax.div(seq, 2)
    z, x = lax.div(pair, wide), lax.rem(pair, wide)
    partner = seq + 1 - 2 * core
    half = deep // 2
    steps = sorted(range(1, wide), key=lambda k: min(k, wide - k))

    def at_z(j):
        return (lax.rem(z + j, deep) * wide + x) * 2 + core

    def at_x(k):
        return (z * wide + lax.rem(x + k, wide)) * 2 + core

    barrier = pltpu.get_barrier_semaphore()

    def both_ways(act):
        act(half)

        def body(i, carry):
            act(half - i)
            act(half + i)
            return carry

        lax.fori_loop(1, half, body, 0)

    both_ways(
        lambda j: pl.semaphore_signal(barrier, inc=1, device_id={"seq": at_z(j)}, device_id_type=MESH)
    )
    for k in range(1, wide):
        pl.semaphore_signal(barrier, inc=1, device_id={"seq": at_x(k)}, device_id_type=MESH)
    for off in (1, 2, 3):
        pl.semaphore_signal(barrier, inc=1, device_id={"head": peer(off)}, device_id_type=MESH)
    for side in (left, right, partner):
        pl.semaphore_signal(barrier, inc=1, device_id={"seq": side}, device_id_type=MESH)

    for h in range(HEADS_ALL):
        gain_ref[h] = gain_all[h * PART : (h + 1) * PART][None, :]
    len_row[...] = jnp.zeros_like(len_row)
    len_row[0:1, 0 : len_ref.shape[1]] = len_ref[...].astype(f32)
    rows_i = lax.broadcasted_iota(jnp.int32, (F, F), 0)
    cols_i = lax.broadcasted_iota(jnp.int32, (F, F), 1)
    pl.semaphore_wait(barrier, deep + wide + 4)

    def across(k):
        return remote(
            loader.at[:, lax.rem(x + k, wide)], xin.at[x], x_send.at[k], x_recv.at[k], {"seq": at_x(k)}
        )

    def held(k, layer):
        came = lax.rem(x + wide - k, wide)
        return xin.at[came, layer] if k else loader.at[layer, x]

    def far(j, k):
        came = lax.rem(x + wide - k, wide)
        return remote(
            held(k, lax.rem(z + j, deep)), arr.at[z, came],
            z_send.at[k, j], z_recv.at[k, j], {"seq": at_z(j)},
        )

    def keep(k):
        return pltpu.make_async_copy(held(k, z), arr.at[z, lax.rem(x + wide - k, wide)], l_sem.at[k])

    def pass_on(j, k):
        layer, came = lax.rem(z + deep - j, deep), lax.rem(x + wide - k, wide)
        return remote(
            arr.at[layer, came], par.at[layer, came], f_send.at[k, j], f_recv.at[k, j], {"seq": partner}
        )

    for k in steps[::-1]:
        across(k).start()
    both_ways(lambda j: far(j, 0).start())
    keep(0).start()
    for k in steps:
        across(k).wait_recv()
        both_ways(lambda j: far(j, k).start())
        keep(k).start()

    lens = len_row[0:1, :]
    ends_col = jnp.sum(jnp.where(cols_i <= rows_i, lens, 0.0), axis=1, keepdims=True)
    lens_col = jnp.transpose(jnp.broadcast_to(lens, (LANES, F)))[:, 0:1]
    ends_row = jnp.sum(jnp.where(rows_i <= cols_i, lens_col, 0.0), axis=0, keepdims=True)
    total = (seq_count * F) * 1.0
    first = (seq * F - WIN).astype(f32)
    for b in range(3):
        place_row = lax.broadcasted_iota(jnp.int32, (1, F), 1).astype(f32) + (first + b * F)
        inside = (place_row >= 0.0) & (place_row < total)
        count = jnp.sum((ends_col <= place_row).astype(f32), axis=0, keepdims=True)
        seg_row[0:1, b * F : (b + 1) * F] = jnp.where(inside, count, -1.0)
        place_col = lax.broadcasted_iota(jnp.int32, (F, 1), 0).astype(f32) + (first + b * F)
        inside = (place_col >= 0.0) & (place_col < total)
        count = jnp.sum((ends_row <= place_col).astype(f32), axis=1, keepdims=True)
        seg_col[b * F : (b + 1) * F, :] = jnp.broadcast_to(jnp.where(inside, count, -1.0), (F, LANES))

    own_seg = seg_col[WIN : WIN + F, 0:1]
    for b in range(3):
        ok = seg_row[0:1, b * F : (b + 1) * F] == own_seg
        if b == 0:
            ok = ok & (cols_i >= rows_i)
        if b == 2:
            ok = ok & (cols_i < rows_i)
        bias[b] = jnp.where(ok, 0.0, -jnp.inf)

    lane = lax.broadcasted_iota(jnp.int32, (1, LANES), 1)
    mf = [(lane < HEAD_DIM).astype(f32), (lane >= HEAD_DIM).astype(f32)]
    mb = [m.astype(bf16) for m in mf]

    chosen = (lax.broadcasted_iota(jnp.int32, (8, seq_count), 1) == seq).astype(f32).astype(bf16)
    counts = mm_nt(chosen, plan_ref[...].astype(f32).astype(bf16)).astype(bf16)
    lower = lax.broadcasted_iota(jnp.int32, (seq_count, seq_count), 0)
    upper = lax.broadcasted_iota(jnp.int32, (seq_count, seq_count), 1)
    starts = mm(counts, (lower < upper).astype(f32).astype(bf16)).astype(bf16)
    loader_row = lax.broadcasted_iota(jnp.int32, (seq_count, slots), 0)
    slot_pair = lax.shift_right_logical(
        lax.broadcasted_iota(jnp.int32, (seq_count, slots), 1), jnp.int32(tile.bit_length() - 1)
    )
    slot_row = lax.broadcasted_iota(jnp.int32, (1, slots), 1)
    slot_core = lax.shift_right_logical(slot_row, jnp.int32(capacity.bit_length() - 1)) & 1
    within = (slot_row & (capacity - 1)).astype(f32)
    frame_rows = lax.broadcasted_iota(jnp.int32, (F, slots), 0).astype(f32)
    for which, parity in ((0, core), (1, 1 - core)):
        spread = (loader_row == 2 * slot_pair + parity).astype(f32).astype(bf16)
        count = mm(counts, spread)[0:1, :]
        start = mm(starts, spread)[0:1, :]
        target = jnp.where((slot_core == core) & (within < count), start + within, -1.0)
        hot[which] = (frame_rows == target).astype(f32).astype(bf16)

    for k in [0] + steps:
        keep(k).wait()
        pass_on(0, k).start()

        def land(j):
            far(j, k).wait_recv()
            pass_on(j, k).start()

        both_ways(land)
    picked = mm(hot[0], arr[...].reshape(slots, PART))
    for k in [0] + steps:
        pass_on(0, k).wait_recv()
        both_ways(lambda j: pass_on(j, k).wait_recv())
    frame_ref[...] = (picked + mm(hot[1], par[...].reshape(slots, PART))).astype(bf16)

    low, high = pl.ds(0, F // 2), pl.ds(F // 2, F // 2)
    up, down_by = {"head": peer(1)}, {"head": peer(3)}

    def gather_copy(i, src, slot, rows, where):
        return remote(src, gath.at[slot, rows, :], ag_send.at[i], ag_recv.at[i], where)

    gathers = [
        gather_copy(0, frame_ref.at[low, :], me, low, up),
        gather_copy(1, frame_ref.at[high, :], me, high, up),
        gather_copy(2, frame_ref.at[high, :], me, high, down_by),
        gather_copy(3, frame_ref.at[low, :], me, low, down_by),
        gather_copy(4, gath.at[peer(3), low, :], peer(3), low, up),
        gather_copy(5, gath.at[peer(1), high, :], peer(1), high, down_by),
    ]
    for i in (0, 2, 1, 3):
        gathers[i].start()
    gath[me] = frame_ref[...]
    gathers[0].wait_recv()
    gathers[4].start()
    gathers[2].wait_recv()
    gathers[5].start()
    for i in (1, 3, 4, 5):
        gathers[i].wait_recv()

    def norm_rows(r, carry):
        rows = pl.ds(pl.multiple_of(r * 32, 32), 32)
        xs = [gath[h, rows, :].astype(f32) for h in range(HEADS_ALL)]
        total = sum(jnp.sum(x, axis=1, keepdims=True) for x in xs)
        mean = total * (1.0 / (HEADS_ALL * PART))
        xs = [x - mean for x in xs]
        square = sum(jnp.sum(x * x, axis=1, keepdims=True) for x in xs)
        inv = lax.rsqrt(square * (1.0 / (HEADS_ALL * PART)) + EPSILON)
        inv_ref[rows, :] = jnp.broadcast_to(inv, (32, LANES))
        for h in range(HEADS_ALL):
            u = xs[h] * inv
            unit[h, rows, :] = u
            normed[rows, h * PART : (h + 1) * PART] = (u * gain_ref[h]).astype(bf16)
        return carry

    lax.fori_loop(0, F // 32, norm_rows, 0)

    halos = []
    for which, weight in ((0, wk), (1, wv)):
        loads[which].wait()
        rows = mm(normed[...], weight[...]).astype(bf16)
        for g in range(GROUPS):
            kv[1, which, g] = rows[:, g * LANES : (g + 1) * LANES]
        halos.append(
            remote(kv.at[1, which], kv.at[2, which], kv_send.at[which, 0], kv_recv.at[which, 0], {"seq": left})
        )
        halos.append(
            remote(kv.at[1, which], kv.at[0, which], kv_send.at[which, 1], kv_recv.at[which, 1], {"seq": right})
        )
        halos[-2].start()
        halos[-1].start()
    loads[2].wait()
    rows = mm(normed[...], wq[...]).astype(bf16)
    for g in range(GROUPS):
        qs[g] = rows[:, g * LANES : (g + 1) * LANES]

    def own_scores(g, carry):
        for sub in range(2):
            wts[2 * g + sub, 1] = mm_nt(qs[g] * mb[sub], kv[1, 0, g]) * scale + bias[1]
        return carry

    lax.fori_loop(0, GROUPS, own_scores, 0)
    for copy in halos[:2]:
        copy.wait_recv()

    def weigh(g, carry):
        for sub in range(2):
            qm = qs[g] * mb[sub]
            score = [
                mm_nt(qm, kv[0, 0, g]) * scale + bias[0],
                wts[2 * g + sub, 1],
                mm_nt(qm, kv[2, 0, g]) * scale + bias[2],
            ]
            top = jnp.maximum(jnp.maximum(score[0], score[1]), score[2])
            top = jnp.max(top, axis=1, keepdims=True)
            lifted = [jnp.exp(x - top) for x in score]
            total = jnp.sum(lifted[0] + lifted[1] + lifted[2], axis=1, keepdims=True)
            inv = 1.0 / total
            for b in range(3):
                w = lifted[b] * inv
                wts[2 * g + sub, b] = w
                wlow[2 * g + sub, b] = w.astype(bf16)
        return carry

    lax.fori_loop(0, GROUPS, weigh, 0)
    for copy in halos[2:]:
        copy.wait_recv()

    def attend(g, carry):
        parts = []
        for sub in range(2):
            acc = mm(wlow[2 * g + sub, 0], kv[0, 1, g])
            for b in (1, 2):
                acc = acc + mm(wlow[2 * g + sub, b], kv[b, 1, g])
            parts.append(acc * mf[sub])
        both = parts[0] + parts[1]
        att[g] = both
        columns = pl.ds(pl.multiple_of(g * LANES, LANES), LANES)
        res = (frame_ref[:, columns].astype(f32) + both).astype(bf16)
        res_low[g] = res
        res_ext[g, PAD : PAD + F, :] = res.astype(f32)
        return carry

    lax.fori_loop(0, GROUPS, attend, 0)

    def edges(low, halo, send, recv):
        return [
            remote(low.at[:, 0:PAD, :], halo.at[1], send.at[0], recv.at[0], {"seq": left}),
            remote(low.at[:, F - PAD : F, :], halo.at[0], send.at[1], recv.at[1], {"seq": right}),
        ]

    def place(halo, ext):
        for g in range(GROUPS):
            ext[g, 0:PAD, :] = halo[0, g].astype(f32)
            ext[g, PAD + F : 2 * PAD + F, :] = halo[1, g].astype(f32)

    res_edges = edges(res_low, res_halo, rh_send, rh_recv)
    for copy in res_edges:
        copy.start()

    def taps(ext, r, mirrored):
        base = seg_col[WIN + r : WIN + r + CHUNK, :]
        acc = [jnp.zeros((CHUNK, LANES), f32) for _ in range(GROUPS)]
        for t in range(KS):
            shift = (HALF_K - t) if mirrored else (t - HALF_K)
            same = seg_col[WIN + r + shift : WIN + r + shift + CHUNK, :] == base
            for g in range(GROUPS):
                term = ext[g, PAD + r + shift : PAD + r + shift + CHUNK, :]
                term = term * cw_ref[t : t + 1, g * LANES : (g + 1) * LANES]
                acc[g] = acc[g] + jnp.where(same, term, 0.0)
        return acc

    def forward_conv(starts):
        for r in starts:
            for g, conv in enumerate(taps(res_ext, r, False)):
                columns = slice(g * LANES, (g + 1) * LANES)
                gate = lax.logistic(conv)
                out_ref[r : r + CHUNK, columns] = (
                    res_ext[g, PAD + r : PAD + r + CHUNK, :] + conv * gate
                ).astype(bf16)
                up = cot_ref[r : r + CHUNK, columns].astype(f32)
                gc = (up * gate * (1.0 + conv * (1.0 - gate))).astype(bf16)
                gc_low[g, r : r + CHUNK, :] = gc
                gc_ext[g, PAD + r : PAD + r + CHUNK, :] = gc.astype(f32)

    def backward_conv(starts):
        for r in starts:
            for g, moved in enumerate(taps(gc_ext, r, True)):
                columns = slice(g * LANES, (g + 1) * LANES)
                up = cot_ref[r : r + CHUNK, columns].astype(f32)
                gres[g, r : r + CHUNK, :] = (up + moved).astype(bf16)

    inner = (CHUNK, 2 * CHUNK)
    outer = (0, 3 * CHUNK)
    forward_conv(inner)
    for copy in res_edges:
        copy.wait_recv()
    place(res_halo, res_ext)
    forward_conv(outer)
    gc_edges = edges(gc_low, gc_halo, gh_send, gh_recv)
    for copy in gc_edges:
        copy.start()
    backward_conv(inner)
    for copy in gc_edges:
        copy.wait_recv()
    place(gc_halo, gc_ext)
    backward_conv(outer)

    def kv_grad_copies(g):
        return [
            remote(dsend.at[0, g], drecv.at[1, g], d_send.at[0, g], d_recv.at[1, g], {"seq": left}),
            remote(dsend.at[1, g], drecv.at[0, g], d_send.at[1, g], d_recv.at[0, g], {"seq": right}),
        ]

    rows_lane = lax.broadcasted_iota(jnp.int32, (LANES, 1), 0)
    mt = [(rows_lane < HEAD_DIM).astype(f32), (rows_lane >= HEAD_DIM).astype(f32)]

    def attend_back(blocks):
        def body(g, carry):
            q_turned = jnp.transpose(qs[g].astype(f32))
            g_turned = jnp.transpose(gres[g].astype(f32))
            gq = []
            dk = {b: None for b in blocks}
            dv = {b: None for b in blocks}
            for sub in range(2):
                gm = gres[g] * mb[sub]
                qt = (q_turned * mt[sub]).astype(bf16)
                gt = (g_turned * mt[sub]).astype(bf16)
                delta = jnp.sum(gm.astype(f32) * att[g], axis=1, keepdims=True)
                acc = None
                for b in blocks:
                    gw = mm_nt(gm, kv[b, 1, g])
                    ds = (wts[2 * g + sub, b] * (gw - delta) * scale).astype(bf16)
                    term = mm(ds, kv[b, 0, g])
                    acc = term if acc is None else acc + term
                    dkt = mm(qt, ds)
                    dvt = mm(gt, wlow[2 * g + sub, b])
                    dk[b] = dkt if dk[b] is None else dk[b] + dkt
                    dv[b] = dvt if dv[b] is None else dv[b] + dvt
                gq.append(acc * mf[sub])
            gq = gq[0] + gq[1]
            columns = pl.ds(pl.multiple_of(g * LANES, LANES), LANES)
            if blocks == (1,):
                dq_ref[:, columns] = (gq + dq_part[g]).astype(bf16)
                down[g, 0] = dk[1]
                down[g, 1] = dv[1]
            else:
                dq_part[g] = gq
                for slot, b in ((0, 0), (1, 2)):
                    dsend[slot, g, 0] = dk[b].astype(bf16)
                    dsend[slot, g, 1] = dv[b].astype(bf16)
                for copy in kv_grad_copies(g):
                    copy.start()
            return carry

        lax.fori_loop(0, GROUPS, body, 0)

    attend_back((0, 2))
    attend_back((1,))

    def weight_rows(ref, off):
        return ref[pl.ds(pl.multiple_of(peer(off) * PART, PART), PART), :]

    for off in (2, 1, 3, 0):
        pacc[off] = mm_nt(dq_ref[...], weight_rows(wq, off))

    for g in range(GROUPS):
        for copy in kv_grad_copies(g):
            copy.wait_recv()
        for which, dst in ((0, dkb), (1, dvb)):
            summed = down[g, which] + drecv[0, g, which].astype(f32) + drecv[1, g, which].astype(f32)
            dst[:, g * LANES : (g + 1) * LANES] = jnp.transpose(summed).astype(bf16)

    row_sum = jnp.zeros((F, 1), f32)
    row_dot = jnp.zeros((F, 1), f32)
    exchanges = []
    for off in (2, 1, 3, 0):
        part = pacc[off] + mm_nt(dkb[...], weight_rows(wk, off)) + mm_nt(dvb[...], weight_rows(wv, off))
        part = part * gain_ref[peer(off)]
        row_sum = row_sum + jnp.sum(part, axis=1, keepdims=True)
        row_dot = row_dot + jnp.sum(part * unit[peer(off)], axis=1, keepdims=True)
        if off:
            psend[off - 1] = part.astype(bf16)
            copy = remote(
                psend.at[off - 1], precv.at[off - 1], p_send.at[off - 1], p_recv.at[off - 1], {"head": peer(off)}
            )
            copy.start()
            exchanges.append(copy)
        else:
            pacc[0] = part

    lanes = lax.broadcasted_iota(jnp.int32, (F, LANES), 1)
    packed = jnp.where(lanes == 0, row_sum, jnp.where(lanes == 1, row_dot, 0.0))
    ssend[...] = jnp.transpose(packed)[0:8, :]
    for off in (2, 1, 3):
        copy = remote(ssend, srecv.at[off - 1], s_send.at[off - 1], s_recv.at[off - 1], {"head": peer(off)})
        copy.start()
        exchanges.append(copy)
    for copy in exchanges:
        copy.wait_recv()
    sums = ssend[...] + srecv[0] + srecv[1] + srecv[2]
    sums = jnp.transpose(jnp.concatenate([sums] * (LANES // 8), axis=0)) * (1.0 / (HEADS_ALL * PART))
    inv_ref[:, 1:2] = sums[:, 0:1]
    inv_ref[:, 2:3] = sums[:, 1:2]

    def finish(r, carry):
        rows = pl.ds(pl.multiple_of(r * 32, 32), 32)
        scaled = pacc[0, rows, :]
        for i in range(3):
            scaled = scaled + precv[i, rows, :].astype(f32)
        through = inv_ref[rows, 0:1] * (
            scaled - inv_ref[rows, 1:2] - unit[me, rows, :] * inv_ref[rows, 2:3]
        )
        for g in range(GROUPS):
            columns = slice(g * LANES, (g + 1) * LANES)
            grad_ref[rows, columns] = (gres[g, rows, :].astype(f32) + through[:, columns]).astype(bf16)
        return carry

    lax.fori_loop(0, F // 32, finish, 0)

    for k in [0] + steps:
        if k:
            across(k).wait_send()

        def drain(j):
            far(j, k).wait_send()
            pass_on(j, k).wait_send()

        both_ways(drain)
        pass_on(0, k).wait_send()
    for copy in gathers + halos + res_edges + gc_edges + exchanges:
        copy.wait_send()
    for g in range(GROUPS):
        for copy in kv_grad_copies(g):
            copy.wait_send()


def copy_kernel(a_ref, b_ref, c_ref, d_ref, held, came, gone):
    ins = [pltpu.make_async_copy(r, held.at[i], came.at[i]) for i, r in enumerate((a_ref, b_ref))]
    outs = [pltpu.make_async_copy(held.at[i], r, gone.at[i]) for i, r in enumerate((c_ref, d_ref))]
    for copy in ins:
        copy.start()
    for i in range(2):
        ins[i].wait()
        outs[i].start()
    for copy in outs:
        copy.wait()


def hand_out(results):
    hbm = pl.BlockSpec(memory_space=pl.ANY)
    shape = jax.ShapeDtypeStruct((F, PART), jnp.bfloat16)
    dma = pltpu.SemaphoreType.DMA
    return pl.pallas_call(
        copy_kernel,
        out_shape=(shape, shape),
        in_specs=[hbm, hbm],
        out_specs=(hbm, hbm),
        scratch_shapes=[pltpu.VMEM((2, F, PART), jnp.bfloat16), dma((2,)), dma((2,))],
    )(*results)


def block_call(loader_rows, plan, lengths, gain, wq, wk, wv, conv_weight, cotangent):
    f32, bf16 = jnp.float32, jnp.bfloat16
    seq_count = lax.axis_size("seq")
    span = F + 2 * WIN
    pairs = seq_count // 2
    tile = loader_rows.shape[0] // pairs
    slots = pairs * tile
    wide = 4 if pairs > 8 else 2
    deep = pairs // wide
    loader = loader_rows.reshape(deep, wide, tile, PART)
    vmem = pl.BlockSpec(memory_space=pltpu.VMEM)
    hbm = pl.BlockSpec(memory_space=pl.ANY)
    v = pltpu.VMEM
    dma = pltpu.SemaphoreType.DMA
    shape = jax.ShapeDtypeStruct((F, PART), bf16)
    return pl.pallas_call(
        block_kernel,
        out_shape=(shape, shape),
        in_specs=[vmem] * 5 + [hbm] * 4,
        out_specs=(vmem, vmem),
        scratch_shapes=[
            v((wide, deep, tile, PART), bf16),
            v((deep, wide, tile, PART), bf16),
            v((deep, wide, tile, PART), bf16),
            v((2, F, slots), bf16),
            v((8, F), f32),
            v((8, span), f32),
            v((span, LANES), f32),
            v((HEADS_ALL, 1, PART), f32),
            v((F, PART), bf16),
            v((HEADS_ALL, F, PART), bf16),
            v((HEADS_ALL, F, PART), f32),
            v((F, HEADS_ALL * PART), bf16),
            v((F, LANES), f32),
            v((HEADS_ALL * PART, PART), bf16),
            v((HEADS_ALL * PART, PART), bf16),
            v((HEADS_ALL * PART, PART), bf16),
            v((3, 2, GROUPS, F, LANES), bf16),
            v((GROUPS, F, LANES), bf16),
            v((3, F, F), f32),
            v((2 * GROUPS, 3, F, F), f32),
            v((2 * GROUPS, 3, F, F), bf16),
            v((GROUPS, F, LANES), f32),
            v((GROUPS, F, LANES), bf16),
            v((GROUPS, F + 2 * PAD, LANES), f32),
            v((2, GROUPS, PAD, LANES), bf16),
            v((GROUPS, F, LANES), bf16),
            v((GROUPS, F + 2 * PAD, LANES), f32),
            v((2, GROUPS, PAD, LANES), bf16),
            v((GROUPS, F, LANES), bf16),
            v((F, PART), bf16),
            v((GROUPS, F, LANES), f32),
            v((2, GROUPS, 2, LANES, F), bf16),
            v((2, GROUPS, 2, LANES, F), bf16),
            v((GROUPS, 2, LANES, F), f32),
            v((F, PART), bf16),
            v((F, PART), bf16),
            v((HEADS_ALL, F, PART), f32),
            v((3, F, PART), bf16),
            v((3, F, PART), bf16),
            v((8, F), f32),
            v((3, 8, F), f32),
            dma((wide, deep)),
            dma((wide, deep)),
            dma((wide,)),
            dma((wide,)),
            dma((wide,)),
            dma((wide, deep)),
            dma((wide, deep)),
            dma((3,)),
            dma((6,)),
            dma((6,)),
            dma((2, 2)),
            dma((2, 2)),
            dma((2,)),
            dma((2,)),
            dma((2,)),
            dma((2,)),
            dma((2, GROUPS)),
            dma((2, GROUPS)),
            dma((3,)),
            dma((3,)),
            dma((3,)),
            dma((3,)),
        ],
        compiler_params=pltpu.CompilerParams(
            collective_id=0, has_side_effects=True, vmem_limit_bytes=56 * 1024 * 1024
        ),
    )(plan, lengths[None, :], gain, conv_weight, cotangent, loader, wq, wk, wv)


def on_device(loader_rows, plan, lengths, gain, wq, wk, wv, conv_weight, cotangent):
    return hand_out(block_call(loader_rows, plan, lengths, gain, wq, wk, wv, conv_weight, cotangent))


def solution(mesh):
    placed = (
        P("seq", "head"),
        P(),
        P(),
        P(),
        P(None, "head"),
        P(None, "head"),
        P(None, "head"),
        P(None, "head"),
        P("seq", "head"),
    )
    return jax.shard_map(
        on_device,
        mesh=mesh,
        in_specs=placed,
        out_specs=(P("seq", "head"), P("seq", "head")),
        check_vma=False,
    )
```

```python
import math

import jax
import jax.numpy as jnp
from jax import lax
from jax.experimental import pallas as pl
from jax.experimental.pallas import tpu as pltpu
from jax.sharding import PartitionSpec as P

HEAD_DIM = 64
KS = 31
HALF_K = 15
WIN = 256
F = 256
PART = 384
GROUPS = 3
LANES = 128
HEADS_ALL = 4
CHUNK = 64
PAD = 16


EPSILON = 1e-05
MESH = pl.DeviceIdType.MESH


def mm(a, b):
    return jnp.dot(a, b, preferred_element_type=jnp.float32)


def mm_nt(a, b):
    return lax.dot_general(a, b, (((1,), (1,)), ((), ())), preferred_element_type=jnp.float32)


def block_kernel(
    plan_ref, len_ref, gain_all, cw_ref, cot_ref, loader, wq_hbm, wk_hbm, wv_hbm,
    out_ref, grad_ref,
    xin, arr, par, hot, len_row, seg_row, seg_col, gain_ref, frame_ref, gath, unit, normed, inv_ref, wq, wk, wv, kv, qs, bias, wts, wlow, att,
    res_low, res_ext, res_halo, gc_low, gc_ext, gc_halo, gres,
    dq_ref, dq_part, dsend, drecv, down, dkb, dvb, pacc, psend, precv, ssend, srecv,
    z_send, z_recv, x_send, x_recv, l_sem, f_send, f_recv, w_sem, ag_send, ag_recv, kv_send, kv_recv, rh_send, rh_recv, gh_send, gh_recv,
    d_send, d_recv, p_send, p_recv, s_send, s_recv,
):
    seq_count = lax.axis_size("seq")
    me = lax.axis_index("head")
    seq = lax.axis_index("seq")
    right = lax.rem(seq + 1, seq_count)
    left = lax.rem(seq + seq_count - 1, seq_count)
    scale = 1.0 / math.sqrt(HEAD_DIM)
    f32, bf16 = jnp.float32, jnp.bfloat16

    def peer(off):
        return lax.rem(me + off, HEADS_ALL)

    def remote(src, dst, send, recv, where):
        return pltpu.make_async_remote_copy(
            src_ref=src, dst_ref=dst, send_sem=send, recv_sem=recv, device_id=where, device_id_type=MESH
        )

    loads = [
        pltpu.make_async_copy(src, dst, w_sem.at[i])
        for i, (src, dst) in enumerate(((wk_hbm, wk), (wv_hbm, wv), (wq_hbm, wq)))
    ]
    for copy in loads:
        copy.start()

    deep, wide, tile = loader.shape[0], loader.shape[1], loader.shape[2]
    slots, capacity = deep * wide * tile, tile // 2
    core = lax.rem(seq, 2)
    pair = lax.div(seq, 2)
    z, x = lax.div(pair, wide), lax.rem(pair, wide)
    partner = seq + 1 - 2 * core
    half = deep // 2
    steps = sorted(range(1, wide), key=lambda k: min(k, wide - k))

    def at_z(j):
        return (lax.rem(z + j, deep) * wide + x) * 2 + core

    def at_x(k):
        return (z * wide + lax.rem(x + k, wide)) * 2 + core

    barrier = pltpu.get_barrier_semaphore()

    def both_ways(act):
        act(half)

        def body(i, carry):
            act(half - i)
            act(half + i)
            return carry

        lax.fori_loop(1, half, body, 0)

    both_ways(
        lambda j: pl.semaphore_signal(barrier, inc=1, device_id={"seq": at_z(j)}, device_id_type=MESH)
    )
    for k in range(1, wide):
        pl.semaphore_signal(barrier, inc=1, device_id={"seq": at_x(k)}, device_id_type=MESH)
    for off in (1, 2, 3):
        pl.semaphore_signal(barrier, inc=1, device_id={"head": peer(off)}, device_id_type=MESH)
    for side in (left, right, partner):
        pl.semaphore_signal(barrier, inc=1, device_id={"seq": side}, device_id_type=MESH)

    for h in range(HEADS_ALL):
        gain_ref[h] = gain_all[h * PART : (h + 1) * PART][None, :]
    len_row[...] = jnp.zeros_like(len_row)
    len_row[0:1, 0 : len_ref.shape[1]] = len_ref[...].astype(f32)
    rows_i = lax.broadcasted_iota(jnp.int32, (F, F), 0)
    cols_i = lax.broadcasted_iota(jnp.int32, (F, F), 1)
    pl.semaphore_wait(barrier, deep + wide + 4)

    def across(k):
        return remote(
            loader.at[:, lax.rem(x + k, wide)], xin.at[x], x_send.at[k], x_recv.at[k], {"seq": at_x(k)}
        )

    def held(k, layer):
        came = lax.rem(x + wide - k, wide)
        return xin.at[came, layer] if k else loader.at[layer, x]

    def far(j, k):
        came = lax.rem(x + wide - k, wide)
        return remote(
            held(k, lax.rem(z + j, deep)), arr.at[z, came],
            z_send.at[k, j], z_recv.at[k, j], {"seq": at_z(j)},
        )

    def keep(k):
        return pltpu.make_async_copy(held(k, z), arr.at[z, lax.rem(x + wide - k, wide)], l_sem.at[k])

    def pass_on(j, k):
        layer, came = lax.rem(z + deep - j, deep), lax.rem(x + wide - k, wide)
        return remote(
            arr.at[layer, came], par.at[layer, came], f_send.at[k, j], f_recv.at[k, j], {"seq": partner}
        )

    for k in steps[::-1]:
        across(k).start()
    both_ways(lambda j: far(j, 0).start())
    keep(0).start()
    for k in steps:
        across(k).wait_recv()
        both_ways(lambda j: far(j, k).start())
        keep(k).start()

    lens = len_row[0:1, :]
    ends_col = jnp.sum(jnp.where(cols_i <= rows_i, lens, 0.0), axis=1, keepdims=True)
    lens_col = jnp.transpose(jnp.broadcast_to(lens, (LANES, F)))[:, 0:1]
    ends_row = jnp.sum(jnp.where(rows_i <= cols_i, lens_col, 0.0), axis=0, keepdims=True)
    total = (seq_count * F) * 1.0
    first = (seq * F - WIN).astype(f32)
    for b in range(3):
        place_row = lax.broadcasted_iota(jnp.int32, (1, F), 1).astype(f32) + (first + b * F)
        inside = (place_row >= 0.0) & (place_row < total)
        count = jnp.sum((ends_col <= place_row).astype(f32), axis=0, keepdims=True)
        seg_row[0:1, b * F : (b + 1) * F] = jnp.where(inside, count, -1.0)
        place_col = lax.broadcasted_iota(jnp.int32, (F, 1), 0).astype(f32) + (first + b * F)
        inside = (place_col >= 0.0) & (place_col < total)
        count = jnp.sum((ends_row <= place_col).astype(f32), axis=1, keepdims=True)
        seg_col[b * F : (b + 1) * F, :] = jnp.broadcast_to(jnp.where(inside, count, -1.0), (F, LANES))

    own_seg = seg_col[WIN : WIN + F, 0:1]
    for b in range(3):
        ok = seg_row[0:1, b * F : (b + 1) * F] == own_seg
        if b == 0:
            ok = ok & (cols_i >= rows_i)
        if b == 2:
            ok = ok & (cols_i < rows_i)
        bias[b] = jnp.where(ok, 0.0, -jnp.inf)

    lane = lax.broadcasted_iota(jnp.int32, (1, LANES), 1)
    mf = [(lane < HEAD_DIM).astype(f32), (lane >= HEAD_DIM).astype(f32)]
    mb = [m.astype(bf16) for m in mf]

    chosen = (lax.broadcasted_iota(jnp.int32, (8, seq_count), 1) == seq).astype(f32).astype(bf16)
    counts = mm_nt(chosen, plan_ref[...].astype(f32).astype(bf16)).astype(bf16)
    lower = lax.broadcasted_iota(jnp.int32, (seq_count, seq_count), 0)
    upper = lax.broadcasted_iota(jnp.int32, (seq_count, seq_count), 1)
    starts = mm(counts, (lower < upper).astype(f32).astype(bf16)).astype(bf16)
    loader_row = lax.broadcasted_iota(jnp.int32, (seq_count, slots), 0)
    slot_pair = lax.shift_right_logical(
        lax.broadcasted_iota(jnp.int32, (seq_count, slots), 1), jnp.int32(tile.bit_length() - 1)
    )
    slot_row = lax.broadcasted_iota(jnp.int32, (1, slots), 1)
    slot_core = lax.shift_right_logical(slot_row, jnp.int32(capacity.bit_length() - 1)) & 1
    within = (slot_row & (capacity - 1)).astype(f32)
    frame_rows = lax.broadcasted_iota(jnp.int32, (F, slots), 0).astype(f32)
    for which, parity in ((0, core), (1, 1 - core)):
        spread = (loader_row == 2 * slot_pair + parity).astype(f32).astype(bf16)
        count = mm(counts, spread)[0:1, :]
        start = mm(starts, spread)[0:1, :]
        target = jnp.where((slot_core == core) & (within < count), start + within, -1.0)
        hot[which] = (frame_rows == target).astype(f32).astype(bf16)

    for k in [0] + steps:
        keep(k).wait()
        pass_on(0, k).start()

        def land(j):
            far(j, k).wait_recv()
            pass_on(j, k).start()

        both_ways(land)
    picked = mm(hot[0], arr[...].reshape(slots, PART))
    for k in [0] + steps:
        pass_on(0, k).wait_recv()
        both_ways(lambda j: pass_on(j, k).wait_recv())
    frame_ref[...] = (picked + mm(hot[1], par[...].reshape(slots, PART))).astype(bf16)

    low, high = pl.ds(0, F // 2), pl.ds(F // 2, F // 2)
    up, down_by = {"head": peer(1)}, {"head": peer(3)}

    def gather_copy(i, src, slot, rows, where):
        return remote(src, gath.at[slot, rows, :], ag_send.at[i], ag_recv.at[i], where)

    gathers = [
        gather_copy(0, frame_ref.at[low, :], me, low, up),
        gather_copy(1, frame_ref.at[high, :], me, high, up),
        gather_copy(2, frame_ref.at[high, :], me, high, down_by),
        gather_copy(3, frame_ref.at[low, :], me, low, down_by),
        gather_copy(4, gath.at[peer(3), low, :], peer(3), low, up),
        gather_copy(5, gath.at[peer(1), high, :], peer(1), high, down_by),
    ]
    for i in (0, 2, 1, 3):
        gathers[i].start()
    gath[me] = frame_ref[...]
    gathers[0].wait_recv()
    gathers[4].start()
    gathers[2].wait_recv()
    gathers[5].start()
    for i in (1, 3, 4, 5):
        gathers[i].wait_recv()

    def norm_rows(r, carry):
        rows = pl.ds(pl.multiple_of(r * 32, 32), 32)
        xs = [gath[h, rows, :].astype(f32) for h in range(HEADS_ALL)]
        total = sum(jnp.sum(x, axis=1, keepdims=True) for x in xs)
        mean = total * (1.0 / (HEADS_ALL * PART))
        xs = [x - mean for x in xs]
        square = sum(jnp.sum(x * x, axis=1, keepdims=True) for x in xs)
        inv = lax.rsqrt(square * (1.0 / (HEADS_ALL * PART)) + EPSILON)
        inv_ref[rows, :] = jnp.broadcast_to(inv, (32, LANES))
        for h in range(HEADS_ALL):
            u = xs[h] * inv
            unit[h, rows, :] = u
            normed[rows, h * PART : (h + 1) * PART] = (u * gain_ref[h]).astype(bf16)
        return carry

    lax.fori_loop(0, F // 32, norm_rows, 0)

    halos = []
    for which, weight in ((0, wk), (1, wv)):
        loads[which].wait()
        rows = mm(normed[...], weight[...]).astype(bf16)
        for g in range(GROUPS):
            kv[1, which, g] = rows[:, g * LANES : (g + 1) * LANES]
        halos.append(
            remote(kv.at[1, which], kv.at[2, which], kv_send.at[which, 0], kv_recv.at[which, 0], {"seq": left})
        )
        halos.append(
            remote(kv.at[1, which], kv.at[0, which], kv_send.at[which, 1], kv_recv.at[which, 1], {"seq": right})
        )
        halos[-2].start()
        halos[-1].start()
    loads[2].wait()
    rows = mm(normed[...], wq[...]).astype(bf16)
    for g in range(GROUPS):
        qs[g] = rows[:, g * LANES : (g + 1) * LANES]

    def own_scores(g, carry):
        for sub in range(2):
            wts[2 * g + sub, 1] = mm_nt(qs[g] * mb[sub], kv[1, 0, g]) * scale + bias[1]
        return carry

    lax.fori_loop(0, GROUPS, own_scores, 0)
    for copy in halos[:2]:
        copy.wait_recv()

    def weigh(g, carry):
        for sub in range(2):
            qm = qs[g] * mb[sub]
            score = [
                mm_nt(qm, kv[0, 0, g]) * scale + bias[0],
                wts[2 * g + sub, 1],
                mm_nt(qm, kv[2, 0, g]) * scale + bias[2],
            ]
            top = jnp.maximum(jnp.maximum(score[0], score[1]), score[2])
            top = jnp.max(top, axis=1, keepdims=True)
            lifted = [jnp.exp(x - top) for x in score]
            total = jnp.sum(lifted[0] + lifted[1] + lifted[2], axis=1, keepdims=True)
            inv = 1.0 / total
            for b in range(3):
                w = lifted[b] * inv
                wts[2 * g + sub, b] = w
                wlow[2 * g + sub, b] = w.astype(bf16)
        return carry

    lax.fori_loop(0, GROUPS, weigh, 0)
    for copy in halos[2:]:
        copy.wait_recv()

    def attend(g, carry):
        parts = []
        for sub in range(2):
            acc = mm(wlow[2 * g + sub, 0], kv[0, 1, g])
            for b in (1, 2):
                acc = acc + mm(wlow[2 * g + sub, b], kv[b, 1, g])
            parts.append(acc * mf[sub])
        both = parts[0] + parts[1]
        att[g] = both
        columns = pl.ds(pl.multiple_of(g * LANES, LANES), LANES)
        res = (frame_ref[:, columns].astype(f32) + both).astype(bf16)
        res_low[g] = res
        res_ext[g, PAD : PAD + F, :] = res.astype(f32)
        return carry

    lax.fori_loop(0, GROUPS, attend, 0)

    def edges(low, halo, send, recv):
        return [
            remote(low.at[:, 0:PAD, :], halo.at[1], send.at[0], recv.at[0], {"seq": left}),
            remote(low.at[:, F - PAD : F, :], halo.at[0], send.at[1], recv.at[1], {"seq": right}),
        ]

    def place(halo, ext):
        for g in range(GROUPS):
            ext[g, 0:PAD, :] = halo[0, g].astype(f32)
            ext[g, PAD + F : 2 * PAD + F, :] = halo[1, g].astype(f32)

    res_edges = edges(res_low, res_halo, rh_send, rh_recv)
    for copy in res_edges:
        copy.start()

    def taps(ext, r, mirrored):
        base = seg_col[WIN + r : WIN + r + CHUNK, :]
        acc = [jnp.zeros((CHUNK, LANES), f32) for _ in range(GROUPS)]
        for t in range(KS):
            shift = (HALF_K - t) if mirrored else (t - HALF_K)
            same = seg_col[WIN + r + shift : WIN + r + shift + CHUNK, :] == base
            for g in range(GROUPS):
                term = ext[g, PAD + r + shift : PAD + r + shift + CHUNK, :]
                term = term * cw_ref[t : t + 1, g * LANES : (g + 1) * LANES]
                acc[g] = acc[g] + jnp.where(same, term, 0.0)
        return acc

    def forward_conv(starts):
        for r in starts:
            for g, conv in enumerate(taps(res_ext, r, False)):
                columns = slice(g * LANES, (g + 1) * LANES)
                gate = lax.logistic(conv)
                out_ref[r : r + CHUNK, columns] = (
                    res_ext[g, PAD + r : PAD + r + CHUNK, :] + conv * gate
                ).astype(bf16)
                up = cot_ref[r : r + CHUNK, columns].astype(f32)
                gc = (up * gate * (1.0 + conv * (1.0 - gate))).astype(bf16)
                gc_low[g, r : r + CHUNK, :] = gc
                gc_ext[g, PAD + r : PAD + r + CHUNK, :] = gc.astype(f32)

    def backward_conv(starts):
        for r in starts:
            for g, moved in enumerate(taps(gc_ext, r, True)):
                columns = slice(g * LANES, (g + 1) * LANES)
                up = cot_ref[r : r + CHUNK, columns].astype(f32)
                gres[g, r : r + CHUNK, :] = (up + moved).astype(bf16)

    inner = (CHUNK, 2 * CHUNK)
    outer = (0, 3 * CHUNK)
    forward_conv(inner)
    for copy in res_edges:
        copy.wait_recv()
    place(res_halo, res_ext)
    forward_conv(outer)
    gc_edges = edges(gc_low, gc_halo, gh_send, gh_recv)
    for copy in gc_edges:
        copy.start()
    backward_conv(inner)
    for copy in gc_edges:
        copy.wait_recv()
    place(gc_halo, gc_ext)
    backward_conv(outer)

    def kv_grad_copies(g):
        return [
            remote(dsend.at[0, g], drecv.at[1, g], d_send.at[0, g], d_recv.at[1, g], {"seq": left}),
            remote(dsend.at[1, g], drecv.at[0, g], d_send.at[1, g], d_recv.at[0, g], {"seq": right}),
        ]

    rows_lane = lax.broadcasted_iota(jnp.int32, (LANES, 1), 0)
    mt = [(rows_lane < HEAD_DIM).astype(f32), (rows_lane >= HEAD_DIM).astype(f32)]

    def attend_back(blocks):
        def body(g, carry):
            q_turned = jnp.transpose(qs[g].astype(f32))
            g_turned = jnp.transpose(gres[g].astype(f32))
            gq = []
            dk = {b: None for b in blocks}
            dv = {b: None for b in blocks}
            for sub in range(2):
                gm = gres[g] * mb[sub]
                qt = (q_turned * mt[sub]).astype(bf16)
                gt = (g_turned * mt[sub]).astype(bf16)
                delta = jnp.sum(gm.astype(f32) * att[g], axis=1, keepdims=True)
                acc = None
                for b in blocks:
                    gw = mm_nt(gm, kv[b, 1, g])
                    ds = (wts[2 * g + sub, b] * (gw - delta) * scale).astype(bf16)
                    term = mm(ds, kv[b, 0, g])
                    acc = term if acc is None else acc + term
                    dkt = mm(qt, ds)
                    dvt = mm(gt, wlow[2 * g + sub, b])
                    dk[b] = dkt if dk[b] is None else dk[b] + dkt
                    dv[b] = dvt if dv[b] is None else dv[b] + dvt
                gq.append(acc * mf[sub])
            gq = gq[0] + gq[1]
            columns = pl.ds(pl.multiple_of(g * LANES, LANES), LANES)
            if blocks == (1,):
                dq_ref[:, columns] = (gq + dq_part[g]).astype(bf16)
                down[g, 0] = dk[1]
                down[g, 1] = dv[1]
            else:
                dq_part[g] = gq
                for slot, b in ((0, 0), (1, 2)):
                    dsend[slot, g, 0] = dk[b].astype(bf16)
                    dsend[slot, g, 1] = dv[b].astype(bf16)
                for copy in kv_grad_copies(g):
                    copy.start()
            return carry

        lax.fori_loop(0, GROUPS, body, 0)

    attend_back((0, 2))
    attend_back((1,))

    def weight_rows(ref, off):
        return ref[pl.ds(pl.multiple_of(peer(off) * PART, PART), PART), :]

    for off in (2, 1, 3, 0):
        pacc[off] = mm_nt(dq_ref[...], weight_rows(wq, off))

    for g in range(GROUPS):
        for copy in kv_grad_copies(g):
            copy.wait_recv()
        for which, dst in ((0, dkb), (1, dvb)):
            summed = down[g, which] + drecv[0, g, which].astype(f32) + drecv[1, g, which].astype(f32)
            dst[:, g * LANES : (g + 1) * LANES] = jnp.transpose(summed).astype(bf16)

    row_sum = jnp.zeros((F, 1), f32)
    row_dot = jnp.zeros((F, 1), f32)
    exchanges = []
    for off in (2, 1, 3, 0):
        part = pacc[off] + mm_nt(dkb[...], weight_rows(wk, off)) + mm_nt(dvb[...], weight_rows(wv, off))
        part = part * gain_ref[peer(off)]
        pacc[off] = part
        if off:
            psend[off - 1] = part.astype(bf16)
            copy = remote(
                psend.at[off - 1], precv.at[off - 1], p_send.at[off - 1], p_recv.at[off - 1], {"head": peer(off)}
            )
            copy.start()
            exchanges.append(copy)
    for off in range(HEADS_ALL):
        part = pacc[off]
        row_sum = row_sum + jnp.sum(part, axis=1, keepdims=True)
        row_dot = row_dot + jnp.sum(part * unit[peer(off)], axis=1, keepdims=True)

    lanes = lax.broadcasted_iota(jnp.int32, (F, LANES), 1)
    packed = jnp.where(lanes == 0, row_sum, jnp.where(lanes == 1, row_dot, 0.0))
    ssend[...] = jnp.transpose(packed)[0:8, :]
    for off in (2, 1, 3):
        copy = remote(ssend, srecv.at[off - 1], s_send.at[off - 1], s_recv.at[off - 1], {"head": peer(off)})
        copy.start()
        exchanges.append(copy)
    for copy in exchanges:
        copy.wait_recv()
    sums = ssend[...] + srecv[0] + srecv[1] + srecv[2]
    sums = jnp.transpose(jnp.concatenate([sums] * (LANES // 8), axis=0)) * (1.0 / (HEADS_ALL * PART))
    inv_ref[:, 1:2] = sums[:, 0:1]
    inv_ref[:, 2:3] = sums[:, 1:2]

    def finish(r, carry):
        rows = pl.ds(pl.multiple_of(r * 32, 32), 32)
        scaled = pacc[0, rows, :]
        for i in range(3):
            scaled = scaled + precv[i, rows, :].astype(f32)
        through = inv_ref[rows, 0:1] * (
            scaled - inv_ref[rows, 1:2] - unit[me, rows, :] * inv_ref[rows, 2:3]
        )
        for g in range(GROUPS):
            columns = slice(g * LANES, (g + 1) * LANES)
            grad_ref[rows, columns] = (gres[g, rows, :].astype(f32) + through[:, columns]).astype(bf16)
        return carry

    lax.fori_loop(0, F // 32, finish, 0)

    for k in [0] + steps:
        if k:
            across(k).wait_send()

        def drain(j):
            far(j, k).wait_send()
            pass_on(j, k).wait_send()

        both_ways(drain)
        pass_on(0, k).wait_send()
    for copy in gathers + halos + res_edges + gc_edges + exchanges:
        copy.wait_send()
    for g in range(GROUPS):
        for copy in kv_grad_copies(g):
            copy.wait_send()


def copy_kernel(a_ref, b_ref, c_ref, d_ref, held, came, gone):
    ins = [pltpu.make_async_copy(r, held.at[i], came.at[i]) for i, r in enumerate((a_ref, b_ref))]
    outs = [pltpu.make_async_copy(held.at[i], r, gone.at[i]) for i, r in enumerate((c_ref, d_ref))]
    for copy in ins:
        copy.start()
    for i in range(2):
        ins[i].wait()
        outs[i].start()
    for copy in outs:
        copy.wait()


def hand_out(results):
    hbm = pl.BlockSpec(memory_space=pl.ANY)
    shape = jax.ShapeDtypeStruct((F, PART), jnp.bfloat16)
    dma = pltpu.SemaphoreType.DMA
    return pl.pallas_call(
        copy_kernel,
        out_shape=(shape, shape),
        in_specs=[hbm, hbm],
        out_specs=(hbm, hbm),
        scratch_shapes=[pltpu.VMEM((2, F, PART), jnp.bfloat16), dma((2,)), dma((2,))],
    )(*results)


def block_call(loader_rows, plan, lengths, gain, wq, wk, wv, conv_weight, cotangent):
    f32, bf16 = jnp.float32, jnp.bfloat16
    seq_count = lax.axis_size("seq")
    span = F + 2 * WIN
    pairs = seq_count // 2
    tile = loader_rows.shape[0] // pairs
    slots = pairs * tile
    wide = 4 if pairs > 8 else 2
    deep = pairs // wide
    loader = loader_rows.reshape(deep, wide, tile, PART)
    vmem = pl.BlockSpec(memory_space=pltpu.VMEM)
    hbm = pl.BlockSpec(memory_space=pl.ANY)
    v = pltpu.VMEM
    dma = pltpu.SemaphoreType.DMA
    shape = jax.ShapeDtypeStruct((F, PART), bf16)
    return pl.pallas_call(
        block_kernel,
        out_shape=(shape, shape),
        in_specs=[vmem] * 5 + [hbm] * 4,
        out_specs=(vmem, vmem),
        scratch_shapes=[
            v((wide, deep, tile, PART), bf16),
            v((deep, wide, tile, PART), bf16),
            v((deep, wide, tile, PART), bf16),
            v((2, F, slots), bf16),
            v((8, F), f32),
            v((8, span), f32),
            v((span, LANES), f32),
            v((HEADS_ALL, 1, PART), f32),
            v((F, PART), bf16),
            v((HEADS_ALL, F, PART), bf16),
            v((HEADS_ALL, F, PART), f32),
            v((F, HEADS_ALL * PART), bf16),
            v((F, LANES), f32),
            v((HEADS_ALL * PART, PART), bf16),
            v((HEADS_ALL * PART, PART), bf16),
            v((HEADS_ALL * PART, PART), bf16),
            v((3, 2, GROUPS, F, LANES), bf16),
            v((GROUPS, F, LANES), bf16),
            v((3, F, F), f32),
            v((2 * GROUPS, 3, F, F), f32),
            v((2 * GROUPS, 3, F, F), bf16),
            v((GROUPS, F, LANES), f32),
            v((GROUPS, F, LANES), bf16),
            v((GROUPS, F + 2 * PAD, LANES), f32),
            v((2, GROUPS, PAD, LANES), bf16),
            v((GROUPS, F, LANES), bf16),
            v((GROUPS, F + 2 * PAD, LANES), f32),
            v((2, GROUPS, PAD, LANES), bf16),
            v((GROUPS, F, LANES), bf16),
            v((F, PART), bf16),
            v((GROUPS, F, LANES), f32),
            v((2, GROUPS, 2, LANES, F), bf16),
            v((2, GROUPS, 2, LANES, F), bf16),
            v((GROUPS, 2, LANES, F), f32),
            v((F, PART), bf16),
            v((F, PART), bf16),
            v((HEADS_ALL, F, PART), f32),
            v((3, F, PART), bf16),
            v((3, F, PART), bf16),
            v((8, F), f32),
            v((3, 8, F), f32),
            dma((wide, deep)),
            dma((wide, deep)),
            dma((wide,)),
            dma((wide,)),
            dma((wide,)),
            dma((wide, deep)),
            dma((wide, deep)),
            dma((3,)),
            dma((6,)),
            dma((6,)),
            dma((2, 2)),
            dma((2, 2)),
            dma((2,)),
            dma((2,)),
            dma((2,)),
            dma((2,)),
            dma((2, GROUPS)),
            dma((2, GROUPS)),
            dma((3,)),
            dma((3,)),
            dma((3,)),
            dma((3,)),
        ],
        compiler_params=pltpu.CompilerParams(
            collective_id=0, has_side_effects=True, vmem_limit_bytes=56 * 1024 * 1024
        ),
    )(plan, lengths[None, :], gain, conv_weight, cotangent, loader, wq, wk, wv)


def on_device(loader_rows, plan, lengths, gain, wq, wk, wv, conv_weight, cotangent):
    return hand_out(block_call(loader_rows, plan, lengths, gain, wq, wk, wv, conv_weight, cotangent))


def solution(mesh):
    placed = (
        P("seq", "head"),
        P(),
        P(),
        P(),
        P(None, "head"),
        P(None, "head"),
        P(None, "head"),
        P(None, "head"),
        P("seq", "head"),
    )
    return jax.shard_map(
        on_device,
        mesh=mesh,
        in_specs=placed,
        out_specs=(P("seq", "head"), P("seq", "head")),
        check_vma=False,
    )
```
